512 devices in a mesh: rows: 128 (over z, y, core), vec: 4 (over x).
Axes of the slice: x: 4, y: 8, z: 8, core: 2. Of those that a mesh axis runs over, the one named last changes fastest.
Arguments:
- self_tiles: bfloat16 [1024, 256, 256], P('rows'), may hold values from 0.01 to 1, as said below
- link_tiles: bfloat16 [1024, 3, 256, 256], P('rows'), may hold values from 0.01 to 1, as said below
- links: int32 [1024, 3], replicated, may hold values from 0 to 1023, as said below
- coarse_row: int32 [1024], replicated, may hold values from 0 to 511, as said below
- vectors: float32 [16, 262144], P('vec', 'rows'), may hold values from -70 to 70
- directions: float32 [16, 262144], P('vec', 'rows'), may hold values from -70 to 70
Outputs:
- residual: float32 [16, 262144], P('vec', 'rows')
- corrected: float32 [16, 262144], P('vec', 'rows')
- projected: float32 [48, 48], replicated
The draws below stay inside these ranges and needn't reach their ends.
Inputs may be any that keep to these rules, and one draw needn't show every extreme that they name: For each slot s, links[., s] pairs the row blocks: links[links[b, s], s] = b and links[b, s] != b; the linked block lies on the same slab of 8 blocks as b or on the slab just before or after it (blocks numbered slab by slab). `coarse_row`: each coarse row numbers exactly two row blocks. `self_tiles`: each tile is symmetric, entries positive. link_tiles[b, s] is the transpose of link_tiles[links[b, s], s]; entries positive.
All inputs are finite; a program needn't handle non-finite values.
Results may differ from the reference program's by a relative error of at most 0.0029.
Values may be sent and summed in bfloat16 or wider, within the bound.
No kernel may reach another device: no remote copies, remote signals or barrier semaphores. Data moves between devices by JAX's collectives and lax.ppermute only.
A program may use at most 128 MiB of HBM per device.

```python
import math
import jax
import jax.numpy as jnp
from jax import lax

BS = 256
K = 16
LINKS = 3
RB_DEV = 8
NB = 1024
NC = 512
ROWS = 262144
N_ROWS = 128


def pairing_order(window_key, first_block, length, windows):
    window_keys = jax.random.split(window_key, windows)
    shuffled = jax.vmap(lambda single_key: jax.random.permutation(single_key, length))(window_keys)
    offsets = first_block + jnp.arange(windows, dtype=jnp.int32) * length
    return (shuffled.astype(jnp.int32) + offsets[:, None]).reshape(-1)


def make_links(key):
    link_key = jax.random.fold_in(key, 11)
    columns = []
    for slot_index in range(LINKS):
        slot_key = jax.random.fold_in(link_key, slot_index)
        if slot_index % 2 == 0:
            ordering = pairing_order(slot_key, 0, 2 * RB_DEV, N_ROWS // 2)
        else:
            key_low, key_mid, key_high = jax.random.split(slot_key, 3)
            ordering = jnp.concatenate([pairing_order(key_low, 0, RB_DEV, 1), pairing_order(key_mid, RB_DEV, 2 * RB_DEV, N_ROWS // 2 - 1), pairing_order(key_high, NB - RB_DEV, RB_DEV, 1)])
        paired = ordering.reshape(-1, 2)
        partner = jnp.zeros((NB,), jnp.int32).at[paired[:, 0]].set(paired[:, 1]).at[paired[:, 1]].set(paired[:, 0])
        columns.append(partner)
    return jnp.stack(columns, axis=1).astype(jnp.int32)


def tile_values(tile_key, shape):
    return jnp.exp(jax.random.uniform(tile_key, shape, jnp.float32, math.log(0.01), 0.0))


def draw_links(key, part):
    return make_links(key)


def draw_coarse_row(key, part):
    ordering = jax.random.permutation(jax.random.fold_in(key, 41), NB).astype(jnp.int32)
    return jnp.zeros((NB,), jnp.int32).at[ordering].set(jnp.arange(NB, dtype=jnp.int32) // 2)


def draw_self_tiles(key, part):
    values = tile_values(jax.random.fold_in(key, 21), (NB, BS, BS))
    return (0.5 * (values + jnp.swapaxes(values, 1, 2))).astype(jnp.bfloat16)


def draw_link_tiles(key, part):
    partner = make_links(key)
    blocks = jnp.arange(NB, dtype=jnp.int32)[:, None]
    lower = jnp.minimum(blocks, partner)
    upper = jnp.maximum(blocks, partner)
    pair_id = (lower * NB + upper) * LINKS + jnp.arange(LINKS, dtype=jnp.int32)[None, :]
    tile_key = jax.random.fold_in(key, 31)

    def single(pair_number):
        return tile_values(jax.random.fold_in(tile_key, pair_number), (BS, BS))
    values = jax.vmap(jax.vmap(single))(pair_id)
    flipped = (blocks > partner)[:, :, None, None]
    return jnp.where(flipped, jnp.swapaxes(values, 2, 3), values).astype(jnp.bfloat16)


def vector_draw(key, salt):
    vector_key = jax.random.fold_in(key, salt)
    key_scale, key_noise = jax.random.split(vector_key, 2)
    node_scale = jnp.exp(jax.random.uniform(key_scale, (ROWS,), jnp.float32, 0.0, math.log(10.0)))
    noise = jnp.clip(jax.random.normal(key_noise, (K, ROWS), jnp.float32), -5.0, 5.0)
    return (noise * node_scale[None, :]).astype(jnp.float32)


def draw_vectors(key, part):
    return vector_draw(key, 51)


def draw_directions(key, part):
    return vector_draw(key, 61)


def setup_inputs(seed: int = 0) -> dict:
    keys = jax.random.split(jax.random.key(seed), 7)
    self_tiles = draw_self_tiles(jax.random.fold_in(keys[6], 71), 0)
    link_tiles = draw_link_tiles(jax.random.fold_in(keys[6], 71), 0)
    links = draw_links(jax.random.fold_in(keys[6], 71), 0)
    coarse_row = draw_coarse_row(jax.random.fold_in(keys[6], 71), 0)
    vectors = draw_vectors(jax.random.fold_in(keys[6], 71), 0)
    directions = draw_directions(jax.random.fold_in(keys[6], 71), 0)
    return {"self_tiles": self_tiles, "link_tiles": link_tiles, "links": links, "coarse_row": coarse_row, "vectors": vectors, "directions": directions}


spectral_shift = 0.25
damping = 0.6

def spd_solve(matrix, rhs):
    factor = jnp.linalg.cholesky(matrix)
    return jax.scipy.linalg.cho_solve((factor, True), rhs)

def operate(field, root_degree, self_tiles, link_tiles, links):
    scaled = (field / root_degree).astype(jnp.bfloat16)
    blocked = scaled.reshape(K, NB, BS).astype(jnp.float32)
    summed = jnp.einsum('kbj,bij->kbi', blocked, self_tiles.astype(jnp.float32))
    for link_slot in range(LINKS):
        remote = blocked[:, links[:, link_slot], :]
        summed = summed + jnp.einsum('kbj,bij->kbi', remote, link_tiles[:, link_slot].astype(jnp.float32))
    return field - summed.reshape(K, ROWS) / root_degree

def reference(self_tiles, link_tiles, links, coarse_row, vectors, directions):
    degree = (lax.optimization_barrier(jnp.sum(self_tiles.astype(jnp.float32), axis=2)) + lax.optimization_barrier(jnp.sum(link_tiles.astype(jnp.float32), axis=(1, 3)))).reshape(ROWS)
    root_degree = jnp.sqrt(degree)
    image_x = operate(vectors, root_degree, self_tiles, link_tiles, links)
    image_p = operate(directions, root_degree, self_tiles, link_tiles, links)
    gram_x = jnp.dot(vectors, vectors.T, precision=lax.Precision.HIGHEST)
    cross = jnp.dot(vectors, image_x.T, precision=lax.Precision.HIGHEST)
    ritz_coef = spd_solve(gram_x, cross)
    residual = image_x - jnp.dot(ritz_coef.T, vectors, precision=lax.Precision.HIGHEST)
    self_diag = jnp.diagonal(self_tiles, axis1=1, axis2=2).astype(jnp.float32).reshape(ROWS)
    diag_shift = 1.0 + spectral_shift - self_diag / degree
    first = damping * residual / diag_shift
    r_one = residual - (operate(first, root_degree, self_tiles, link_tiles, links) + spectral_shift * first)
    block_degree = degree.reshape(NB, BS).sum(axis=1)
    agg_degree = jnp.zeros((NC,), jnp.float32).at[coarse_row].add(block_degree)
    self_sum = lax.optimization_barrier(jnp.sum(self_tiles.astype(jnp.float32), axis=(1, 2)))
    link_sum = lax.optimization_barrier(jnp.sum(link_tiles.astype(jnp.float32), axis=(2, 3)))
    tile_sum = jnp.zeros((NC, NC), jnp.float32).at[coarse_row, coarse_row].add(self_sum)
    tile_sum = tile_sum.at[coarse_row[:, None], coarse_row[links]].add(link_sum)
    inv_scale = 1.0 / jnp.sqrt(agg_degree)
    coarse_matrix = ((1.0 + spectral_shift) * jnp.diag(agg_degree) - tile_sum) * inv_scale[:, None] * inv_scale[None, :]
    weighted = (root_degree * r_one).reshape(K, NB, BS).sum(axis=2)
    coarse_rhs = jnp.zeros((K, NC), jnp.float32).at[:, coarse_row].add(weighted) * inv_scale[None, :]
    coarse_error = spd_solve(coarse_matrix, coarse_rhs.T).T
    block_gain = (coarse_error * inv_scale[None, :])[:, coarse_row]
    second = first + (root_degree.reshape(NB, BS)[None] * block_gain[:, :, None]).reshape(K, ROWS)
    after = operate(second, root_degree, self_tiles, link_tiles, links) + spectral_shift * second
    corrected = second + damping * (residual - after) / diag_shift
    image_w = operate(corrected, root_degree, self_tiles, link_tiles, links)
    basis = jnp.concatenate([vectors, corrected, directions], axis=0)
    images = jnp.concatenate([image_x, image_w, image_p], axis=0)
    gram_b = jnp.dot(basis, basis.T, precision=lax.Precision.HIGHEST)
    gram_a = jnp.dot(basis, images.T, precision=lax.Precision.HIGHEST)
    factor = jnp.linalg.cholesky(gram_b)
    half_solved = jax.scipy.linalg.solve_triangular(factor, gram_a, lower=True)
    reduced = jax.scipy.linalg.solve_triangular(factor, half_solved.T, lower=True)
    projected = 0.5 * (reduced + reduced.T)
    return (residual, corrected, projected)
```

```python
import functools
import jax
import jax.numpy as jnp
from jax import lax
from jax.experimental import pallas as pl
from jax.experimental.pallas import tpu as pltpu
from jax.sharding import Mesh, PartitionSpec as P

spectral_shift = 0.25
damping = 0.6
LANE = 128
GROUPS = 4

F32 = jnp.float32
BF16 = jnp.bfloat16
EXACT = lax.Precision.HIGHEST


def nn(left, right, precision=None):
    return lax.dot_general(
        left, right, (((1,), (0,)), ((), ())), precision=precision, preferred_element_type=F32
    )


def nt(left, right, precision=None):
    return lax.dot_general(
        left, right, (((1,), (1,)), ((), ())), precision=precision, preferred_element_type=F32
    )


def tn(left, right, precision=None):
    return lax.dot_general(
        left, right, (((0,), (0,)), ((), ())), precision=precision, preferred_element_type=F32
    )


def iota(shape, dim):
    return lax.broadcasted_iota(jnp.int32, shape, dim)


def run(kernel, inputs, outputs, scratch=(), smem=0):
    in_specs = [
        pl.BlockSpec(memory_space=pltpu.SMEM if i < smem else pltpu.VMEM)
        for i in range(len(inputs))
    ]
    single = not isinstance(outputs, (list, tuple))
    shapes = [outputs] if single else list(outputs)
    specs = [pl.BlockSpec(memory_space=pltpu.VMEM) for _ in shapes]
    return pl.pallas_call(
        kernel,
        in_specs=in_specs,
        out_specs=specs[0] if single else specs,
        out_shape=shapes[0] if single else shapes,
        scratch_shapes=list(scratch),
    )(*inputs)


def arr(shape, dtype=F32):
    return jax.ShapeDtypeStruct(shape, dtype)


def safe(value):
    return jnp.where(value > 0.0, value, 1.0)


def prep_kernel(links_s, coarse_s, start_s, self_t, link_t, nodes, col, info):
    count, size = self_t.shape[0], self_t.shape[1]
    ones = jnp.ones((8, size), BF16)
    diagonal = iota((size, size), 0) == iota((size, size), 1)
    lane = iota((1, LANE), 1)
    for b in range(count):
        own = self_t[b]
        degree = nt(ones, own)[0:1]
        col[0, b : b + 1, :] = degree
        row = jnp.where(lane == 0, jnp.sum(degree, axis=1, keepdims=True), 0.0)
        ids = jnp.where(lane == 4, coarse_s[start_s[0] + b], 0)
        for s in range(3):
            tile = link_t[b, s]
            part = nt(ones, tile)[0:1]
            degree = degree + part
            row = jnp.where(lane == 1 + s, jnp.sum(part, axis=1, keepdims=True), row)
            ids = jnp.where(lane == 5 + s, coarse_s[links_s[b, s]], ids)
            col[1 + s, b : b + 1, :] = jnp.sum(tile.astype(F32), axis=0, keepdims=True)
        diag = jnp.sum(jnp.where(diagonal, own.astype(F32), 0.0), axis=0, keepdims=True)
        nodes[b : b + 1, :] = degree
        nodes[count + b : count + b + 1, :] = 1.0 + spectral_shift - diag / degree
        info[b : b + 1, :] = row + ids.astype(F32)


def apply_tiles(window_s, self_t, link_t, win, b, count):
    acc = nt(win[count + b], self_t[b])
    for s in range(3):
        acc = acc + nt(win[window_s[b, s]], link_t[b, s])
    return acc


def image_kernel(window_s, self_t, link_t, zc, zl, zh, nc, nl, nh, image, gram, win):
    count, size = self_t.shape[0], self_t.shape[1]
    half = zc.shape[0] // 2
    for part, (z, nodes) in enumerate(((zl, nl), (zc, nc), (zh, nh))):
        for b in range(count):
            root = jnp.sqrt(safe(nodes[b : b + 1, :]))
            win[part * count + b] = (z[:, b * size : (b + 1) * size] / root).astype(BF16)
    for b in range(count):
        acc = apply_tiles(window_s, self_t, link_t, win, b, count)
        span = slice(b * size, (b + 1) * size)
        image[:, span] = zc[:, span] - acc / jnp.sqrt(nc[b : b + 1, :])
    z = zc[...]
    img = image[...]
    basis = nt(z, z, EXACT)
    cross = nt(img, z, EXACT)
    mixed = 0.5 * (cross[:half, half:] + nt(z[:half], img[half:], EXACT))
    gram[:, 0:half] = basis[:half, :half]
    gram[:, half : 2 * half] = basis[:half, half:]
    gram[:, 2 * half : 3 * half] = basis[half:, half:]
    gram[:, 3 * half : 4 * half] = cross[:half, :half]
    gram[:, 4 * half : 5 * half] = mixed
    gram[:, 5 * half : 6 * half] = cross[half:, half:]
    gram[:, 6 * half :] = jnp.zeros((half, LANE - 6 * half), F32)


def restrict_kernel(
    window_s, zc, zl, zh, ic, il, ih, nc, nl, nh, col, gram, info, out, win, weighted, packed
):
    count, size = col.shape[1], col.shape[2]
    half = zc.shape[0] // 2
    width = 2 * half
    for part, (z, img, nodes) in enumerate(((zl, il, nl), (zc, ic, nc), (zh, ih, nh))):
        for b in range(count):
            span = slice(b * size, (b + 1) * size)
            root = jnp.sqrt(safe(nodes[b : b + 1, :]))
            shift = nodes[count + b : count + b + 1, :]
            shift = jnp.where(shift == 0.0, 1.0, shift)
            field = jnp.concatenate([z[:half, span], img[:half, span]], axis=0)
            smooth = damping * field / shift
            win[part * count + b] = smooth / root
            if part == 1:
                weighted[b * width : (b + 1) * width, :] = root * (
                    field - (1.0 + spectral_shift) * smooth
                )
    for b in range(count):
        acc = weighted[b * width : (b + 1) * width, :] + col[0, b : b + 1, :] * win[count + b]
        for s in range(3):
            acc = acc + col[1 + s, b : b + 1, :] * win[window_s[b, s]]
        weighted[b * width : (b + 1) * width, :] = acc
    sums = nt(jnp.ones((8, size), F32), weighted[...], EXACT)
    packed[...] = gram[...]
    for b in range(count):
        packed[b : b + 1, LANE - width :] = sums[0:1, b * width : (b + 1) * width]
        packed[count + b : count + b + 1, LANE - width :] = info[b : b + 1, 0:width]
    value = packed[...]
    for i in range(out.shape[0]):
        out[i] = value


def relay_kernel(got, out, packed):
    members, rows, _ = got.shape
    deep = members // GROUPS
    width = LANE // GROUPS
    total = got[0]
    for i in range(1, members):
        total = total + got[i]
    packed[0:rows, :] = total
    for i in range(members):
        g, j = i // deep, i % deep
        at = rows + j * rows
        packed[at : at + rows, g * width : (g + 1) * width] = got[i][:, LANE - width :]
    value = packed[...]
    for i in range(out.shape[0]):
        out[i] = value


def add_kernel(got, out):
    total = got[0]
    for i in range(1, got.shape[0]):
        total = total + got[i]
    for i in range(out.shape[0]):
        out[i] = total


def invert_dense(matrix):
    n = matrix.shape[0]
    rows = iota((n, 1), 0)
    lanes = iota((1, n), 1)
    for k in range(0, n, 2):
        r0, r1 = matrix[k : k + 1, :], matrix[k + 1 : k + 2, :]
        c0, c1 = matrix[:, k : k + 1], matrix[:, k + 1 : k + 2]
        a, b = r0[:, k : k + 1], r0[:, k + 1 : k + 2]
        c, d = r1[:, k : k + 1], r1[:, k + 1 : k + 2]
        scale = 1.0 / (a * d - b * c)
        first, second = lanes == k, lanes == k + 1
        r0 = jnp.where(first, 1.0, jnp.where(second, 0.0, r0))
        r1 = jnp.where(second, 1.0, jnp.where(first, 0.0, r1))
        n0 = (d * r0 - b * r1) * scale
        n1 = (a * r1 - c * r0) * scale
        unit = jnp.where(rows == lanes, 1.0, 0.0)
        rest = jnp.where(first | second, unit, matrix)
        matrix = rest - c0 * n0 - c1 * n1
        matrix = jnp.where(rows == k, n0, jnp.where(rows == k + 1, n1, matrix))
    return matrix


def split3(value):
    high = value.astype(BF16)
    rest = value - high.astype(F32)
    mid = rest.astype(BF16)
    low = (rest - mid.astype(F32)).astype(BF16)
    return high, mid, low


def coarse_kernel(coarse_s, start_s, got, coef, gain, gram, uw, info, mat, hot):
    members, depth, _ = got.shape
    rows = 16
    half = rows
    deep = (depth - rows) // rows
    width = LANE // GROUPS
    nc = mat.shape[0]
    count = coarse_s.shape[0]
    total = got[0, 0:rows]
    for y in range(1, members):
        total = total + got[y, 0:rows]
    gram[...] = total
    for y in range(members):
        for j in range(deep):
            at = (y * deep + j) * 8
            src = rows + j * rows
            uw[at : at + 8, :] = got[y, src : src + 8]
            info[at : at + 8, :] = got[y, src + 8 : src + 16]
    blocks = uw.shape[0]
    lanes = iota((blocks, nc), 1)
    agg = jnp.zeros((1, nc), F32)
    tiles = jnp.zeros((nc, nc), F32)
    for g in range(GROUPS):
        at = g * width
        values = [info[:, at + s : at + s + 1] for s in range(4)]
        ids = [info[:, at + 4 + s : at + 5 + s].astype(jnp.int32) for s in range(4)]
        here = lanes == ids[0]
        block_degree = values[0] + values[1] + values[2] + values[3]
        agg = agg + jnp.sum(jnp.where(here, block_degree, 0.0), axis=0, keepdims=True)
        spread = jnp.where(here, values[0], 0.0)
        for s in range(1, 4):
            spread = spread + jnp.where(lanes == ids[s], values[s], 0.0)
        member = jnp.where(here, 1.0, 0.0)
        hot[g] = member
        member = member.astype(BF16)
        for piece in split3(spread):
            tiles = tiles + tn(member, piece)
    same = iota((nc, nc), 0) == iota((nc, nc), 1)
    agg_col = jnp.sum(jnp.where(same, agg, 0.0), axis=1, keepdims=True)
    inv_row = 1.0 / jnp.sqrt(agg)
    inv_col = 1.0 / jnp.sqrt(agg_col)
    mat[...] = (jnp.where(same, (1.0 + spectral_shift) * agg, 0.0) - tiles) * inv_col * inv_row

    block = min(LANE, nc)

    def eliminate(step, _):
        at = pl.multiple_of(step * block, block)
        pivot = invert_dense(mat[pl.ds(at, block), pl.ds(at, block)])
        inside_lane = (iota((1, nc), 1) >= at) & (iota((1, nc), 1) < at + block)
        inside_row = (iota((nc, 1), 0) >= at) & (iota((nc, 1), 0) < at + block)
        shifted = iota((block, nc), 0) + at == iota((block, nc), 1)
        strip = jnp.where(inside_lane, jnp.where(shifted, 1.0, 0.0), mat[pl.ds(at, block), :])
        new_rows = nn(pivot, strip, EXACT)
        column = mat[:, pl.ds(at, block)]
        column = jnp.where(inside_row, 0.0, column)
        kept = jnp.where(inside_lane, 0.0, mat[...])
        mat[...] = kept - nn(column, new_rows, EXACT)
        mat[pl.ds(at, block), :] = new_rows
        return 0

    lax.fori_loop(0, nc // block, eliminate, 0)

    ritz = nn(total[:, 3 * half : 4 * half], invert_dense(total[:, 0:half]), EXACT)
    coef[...] = ritz
    unit = jnp.where(iota((half, half), 0) == iota((half, half), 1), 1.0, 0.0)
    combine = jnp.concatenate([-ritz, unit], axis=1)
    rhs = jnp.zeros((half, nc), F32)
    for g in range(GROUPS):
        block_rhs = nt(combine, uw[:, g * width : (g + 1) * width], EXACT)
        rhs = rhs + nn(block_rhs, hot[g], EXACT)
    error = nn(rhs * inv_row, mat[...], EXACT)
    lifted = error * inv_row
    wide = iota((1, nc), 1)
    picks = []
    for j in range(24):
        at = jnp.clip(start_s[0] - 8 + j, 0, count - 1)
        picks.append(jnp.where(wide == coarse_s[at], 1.0, 0.0))
    picks.append(jnp.zeros((8, nc), F32))
    gain[...] = nt(lifted, jnp.concatenate(picks, axis=0), EXACT)


def correct_kernel(
    window_s, self_t, link_t, zc, zl, zh, ic, il, ih, nc, nl, nh, coef, gain,
    residual, corrected, scaled, win, second,
):
    count, size = self_t.shape[0], self_t.shape[1]
    half = zc.shape[0] // 2
    ritz = coef[...]
    gains = gain[...]
    for part, (z, img, nodes) in enumerate(((zl, il, nl), (zc, ic, nc), (zh, ih, nh))):
        res = img[:half, :] - nn(ritz, z[:half, :], EXACT)
        if part == 1:
            residual[...] = res
        for b in range(count):
            span = slice(b * size, (b + 1) * size)
            root = jnp.sqrt(safe(nodes[b : b + 1, :]))
            shift = nodes[count + b : count + b + 1, :]
            shift = jnp.where(shift == 0.0, 1.0, shift)
            j = part * count + b
            field = damping * res[:, span] / shift + root * gains[:, j : j + 1]
            win[j] = (field / root).astype(BF16)
            if part == 1:
                second[:, span] = field
    for b in range(count):
        span = slice(b * size, (b + 1) * size)
        root = jnp.sqrt(nc[b : b + 1, :])
        shift = nc[count + b : count + b + 1, :]
        acc = apply_tiles(window_s, self_t, link_t, win, b, count)
        field = second[:, span]
        after = field - acc / root + spectral_shift * field
        field = field + damping * (residual[:, span] - after) / shift
        corrected[:, span] = field
        scaled[:, span] = (field / root).astype(BF16)


def search_kernel(window_s, self_t, link_t, w, sc, sl, sh, nc, z, img, out, win, image_w):
    count, size = self_t.shape[0], self_t.shape[1]
    half = w.shape[0]
    for part, s in enumerate((sl, sc, sh)):
        for b in range(count):
            win[part * count + b] = s[:, b * size : (b + 1) * size]
    for b in range(count):
        span = slice(b * size, (b + 1) * size)
        acc = apply_tiles(window_s, self_t, link_t, win, b, count)
        image_w[:, span] = w[:, span] - acc / jnp.sqrt(nc[b : b + 1, :])
    field = w[...]
    field_image = image_w[...]
    zz = z[...]
    value = jnp.concatenate(
        [
            nt(field, zz, EXACT),
            nt(field, field, EXACT),
            0.5 * (nt(field, img[...], EXACT) + nt(field_image, zz, EXACT)),
            nt(field, field_image, EXACT),
            jnp.zeros((half, LANE - 6 * half), F32),
        ],
        axis=1,
    )
    for i in range(out.shape[0]):
        out[i] = value


def project_kernel(got, gram, out):
    h = gram.shape[0]
    n = 3 * h
    new = got[0]
    for i in range(1, got.shape[0]):
        new = new + got[i]
    old = gram[...]
    zero = jnp.zeros((h, h), F32)
    unit = jnp.where(iota((n, n), 0) == iota((n, n), 1), 1.0, 0.0)

    def whole(xx, xp, pp, wx, ww, wp):
        upper = jnp.concatenate(
            [
                jnp.concatenate([0.5 * xx, zero, xp], axis=1),
                jnp.concatenate([wx, 0.5 * ww, wp], axis=1),
                jnp.concatenate([zero, zero, 0.5 * pp], axis=1),
            ],
            axis=0,
        )
        return upper + nt(unit, upper, EXACT)

    def piece(a, i):
        return a[:, i * h : (i + 1) * h]

    gram_b = whole(
        piece(old, 0), piece(old, 1), piece(old, 2), piece(new, 0), piece(new, 2), piece(new, 1)
    )
    gram_a = whole(
        piece(old, 3), piece(old, 4), piece(old, 5), piece(new, 3), piece(new, 5), piece(new, 4)
    )
    work = jnp.concatenate([gram_b, unit], axis=1)
    rows = iota((n, 1), 0)
    for k in range(n):
        pivot = work[k : k + 1, :]
        factor = work[:, k : k + 1] / pivot[:, k : k + 1]
        work = work - jnp.where(rows > k, factor, 0.0) * pivot
    diag = jnp.sum(jnp.where(unit > 0.0, work[:, :n], 0.0), axis=1, keepdims=True)
    inverse = work[:, n:] / jnp.sqrt(diag)
    out[...] = nt(nn(inverse, gram_a, EXACT), inverse, EXACT)


def body(self_tiles, link_tiles, links, coarse_row, vectors, directions):
    count, size = self_tiles.shape[0], self_tiles.shape[1]
    mine = vectors.shape[0]
    slab = count * size
    vec = lax.axis_size("vec")
    k = mine * vec
    row_axes = ("z", "y", "core")
    row_index = lax.axis_index(row_axes)
    row_count = lax.axis_size(row_axes)
    stage_one = ("z", "core")
    n_one = lax.axis_size(stage_one)
    n_two = lax.axis_size("y")
    forward = [(i, i + 1) for i in range(row_count - 1)]
    backward = [(i + 1, i) for i in range(row_count - 1)]

    def halo(a):
        return lax.ppermute(a, row_axes, forward), lax.ppermute(a, row_axes, backward)

    start = row_index * count
    start_s = start.reshape(1).astype(jnp.int32)
    links_s = lax.dynamic_slice_in_dim(links, start, count, 0)
    window_s = links_s - (start - count)

    nodes, col, info = run(
        prep_kernel,
        (links_s, coarse_row, start_s, self_tiles, link_tiles),
        (arr((2 * count, size)), arr((4, count, size)), arr((count, LANE))),
        smem=3,
    )
    both = jnp.broadcast_to(
        jnp.concatenate([vectors, directions], axis=0)[None], (vec, 2 * mine, slab)
    )
    both = lax.all_to_all(both, "vec", 0, 0)
    zc = jnp.swapaxes(both.reshape(vec, 2, mine, slab), 0, 1).reshape(2 * k, slab)
    nl, nh = halo(nodes)
    zl, zh = halo(zc)
    image, gram = run(
        image_kernel,
        (window_s, self_tiles, link_tiles, zc, zl, zh, nodes, nl, nh),
        (arr((2 * k, slab)), arr((k, LANE))),
        scratch=(pltpu.VMEM((3 * count, 2 * k, size), BF16),),
        smem=1,
    )
    il, ih = halo(image[:k])
    sent = run(
        restrict_kernel,
        (window_s, zc, zl, zh, image, il, ih, nodes, nl, nh, col, gram, info),
        arr((n_one, 2 * count, LANE)),
        scratch=(
            pltpu.VMEM((3 * count, 2 * k, size), F32),
            pltpu.VMEM((count * 2 * k, size), F32),
            pltpu.VMEM((2 * count, LANE), F32),
        ),
        smem=1,
    )
    got = lax.all_to_all(sent, stage_one, 0, 0)
    depth = 2 * count * (1 + n_one // GROUPS)
    sent = run(
        relay_kernel,
        (got,),
        arr((n_two, depth, LANE)),
        scratch=(pltpu.VMEM((depth, LANE), F32),),
    )
    got = lax.all_to_all(sent, "y", 0, 0)
    coarse_count = coarse_row.shape[0] // 2
    blocks = n_two * (n_one // GROUPS) * count
    coef, gain, gram = run(
        coarse_kernel,
        (coarse_row, start_s, got),
        (arr((k, k)), arr((k, 32)), arr((k, LANE))),
        scratch=(
            pltpu.VMEM((blocks, LANE), F32),
            pltpu.VMEM((blocks, LANE), F32),
            pltpu.VMEM((coarse_count, coarse_count), F32),
            pltpu.VMEM((GROUPS, blocks, coarse_count), F32),
        ),
        smem=2,
    )
    residual, corrected, scaled = run(
        correct_kernel,
        (
            window_s, self_tiles, link_tiles, zc, zl, zh, image, il, ih,
            nodes, nl, nh, coef, gain,
        ),
        (arr((k, slab)), arr((k, slab)), arr((k, slab), BF16)),
        scratch=(pltpu.VMEM((3 * count, k, size), BF16), pltpu.VMEM((k, slab), F32)),
        smem=1,
    )
    sl, sh = halo(scaled)
    sent = run(
        search_kernel,
        (window_s, self_tiles, link_tiles, corrected, scaled, sl, sh, nodes, zc, image),
        arr((n_one, k, LANE)),
        scratch=(pltpu.VMEM((3 * count, k, size), BF16), pltpu.VMEM((k, slab), F32)),
        smem=1,
    )
    got = lax.all_to_all(sent, stage_one, 0, 0)
    sent = run(add_kernel, (got,), arr((n_two, k, LANE)))
    got = lax.all_to_all(sent, "y", 0, 0)
    projected = run(project_kernel, (got, gram), arr((3 * k, 3 * k)))
    at = lax.axis_index("vec") * mine
    return (
        lax.dynamic_slice_in_dim(residual, at, mine, 0),
        lax.dynamic_slice_in_dim(corrected, at, mine, 0),
        projected,
    )


def row_split(rows):
    return (8, rows // 16, 2) if rows >= 64 else (2, rows // 4, 2)


def solution(mesh):
    z, y, core = row_split(mesh.shape["rows"])
    split = Mesh(
        mesh.devices.reshape(z, y, core, mesh.shape["vec"]), ("z", "y", "core", "vec")
    )
    rows = ("z", "y", "core")
    in_specs = (
        P(rows, None, None),
        P(rows, None, None, None),
        P(),
        P(),
        P("vec", rows),
        P("vec", rows),
    )
    out_specs = (P("vec", rows), P("vec", rows), P())
    return jax.shard_map(body, mesh=split, in_specs=in_specs, out_specs=out_specs, check_vma=False)
```

```python
import jax
import jax.numpy as jnp
from jax import lax
from jax.experimental import pallas as pl
from jax.experimental.pallas import tpu as pltpu
from jax.sharding import Mesh, PartitionSpec as P

spectral_shift = 0.25
damping = 0.6
LANE = 128
GROUPS = 4

F32 = jnp.float32
BF16 = jnp.bfloat16
EXACT = lax.Precision.HIGHEST


def nn(left, right, precision=None):
    return lax.dot_general(
        left, right, (((1,), (0,)), ((), ())), precision=precision, preferred_element_type=F32
    )


def nt(left, right, precision=None):
    return lax.dot_general(
        left, right, (((1,), (1,)), ((), ())), precision=precision, preferred_element_type=F32
    )


def tn(left, right, precision=None):
    return lax.dot_general(
        left, right, (((0,), (0,)), ((), ())), precision=precision, preferred_element_type=F32
    )


def iota(shape, dim):
    return lax.broadcasted_iota(jnp.int32, shape, dim)


def run(kernel, inputs, outputs, scratch=(), smem=0, work=0):
    in_specs = [
        pl.BlockSpec(memory_space=pltpu.SMEM if i < smem else pltpu.VMEM)
        for i in range(len(inputs))
    ]
    single = not isinstance(outputs, (list, tuple))
    shapes = [outputs] if single else list(outputs)
    specs = [pl.BlockSpec(memory_space=pltpu.VMEM) for _ in shapes]
    return pl.pallas_call(
        kernel,
        in_specs=in_specs,
        out_specs=specs[0] if single else specs,
        out_shape=shapes[0] if single else shapes,
        scratch_shapes=list(scratch),
        cost_estimate=pl.CostEstimate(
            flops=work, bytes_accessed=sum(a.size * a.dtype.itemsize for a in inputs), transcendentals=0
        ),
    )(*inputs)


def arr(shape, dtype=F32):
    return jax.ShapeDtypeStruct(shape, dtype)


def safe(value):
    return jnp.where(value > 0.0, value, 1.0)


def prep_kernel(links_s, coarse_s, start_s, self_t, link_t, nodes, col, info):
    count, size = self_t.shape[0], self_t.shape[1]
    ones = jnp.ones((8, size), BF16)
    diagonal = iota((size, size), 0) == iota((size, size), 1)
    lane = iota((1, LANE), 1)
    for b in range(count):
        own = self_t[b]
        degree = nt(ones, own)[0:1]
        col[0, b : b + 1, :] = degree
        row = jnp.where(lane == 0, jnp.sum(degree, axis=1, keepdims=True), 0.0)
        ids = jnp.where(lane == 4, coarse_s[start_s[0] + b], 0)
        for s in range(3):
            tile = link_t[b, s]
            part = nt(ones, tile)[0:1]
            degree = degree + part
            row = jnp.where(lane == 1 + s, jnp.sum(part, axis=1, keepdims=True), row)
            ids = jnp.where(lane == 5 + s, coarse_s[links_s[b, s]], ids)
            col[1 + s, b : b + 1, :] = jnp.sum(tile.astype(F32), axis=0, keepdims=True)
        diag = jnp.sum(jnp.where(diagonal, own.astype(F32), 0.0), axis=0, keepdims=True)
        span = slice(b * size, (b + 1) * size)
        nodes[0:1, span] = degree
        nodes[1:2, span] = 1.0 + spectral_shift - diag / degree
        info[b : b + 1, :] = row + ids.astype(F32)
    nodes[2:8, :] = jnp.zeros((6, nodes.shape[1]), F32)


def pack_kernel(both, nodes, out):
    members, twice, _ = both.shape
    mine = twice // 2
    for v in range(members):
        out[v * mine : (v + 1) * mine, :] = both[v, :mine]
        out[(members + v) * mine : (members + v + 1) * mine, :] = both[v, mine:]
    out[members * twice :, :] = nodes[...]


def apply_tiles(window_s, self_t, link_t, win, b, count):
    acc = nt(win[count + b], self_t[b])
    for s in range(3):
        acc = acc + nt(win[window_s[b, s]], link_t[b, s])
    return acc


def image_kernel(window_s, self_t, link_t, fc, fl, fh, image_x, image_p, gram, win):
    count, size = self_t.shape[0], self_t.shape[1]
    half = image_x.shape[0]
    both = 2 * half
    for part, f in enumerate((fl, fc, fh)):
        for b in range(count):
            span = slice(b * size, (b + 1) * size)
            root = jnp.sqrt(safe(f[both : both + 1, span]))
            win[part * count + b] = (f[:both, span] / root).astype(BF16)
    for b in range(count):
        acc = apply_tiles(window_s, self_t, link_t, win, b, count)
        span = slice(b * size, (b + 1) * size)
        value = fc[:both, span] - acc / jnp.sqrt(fc[both : both + 1, span])
        image_x[:, span] = value[:half]
        image_p[:, span] = value[half:]
    z = fc[:both, :]
    ix = image_x[...]
    ip = image_p[...]
    basis = nt(z, z, EXACT)
    cross = nt(ix, z, EXACT)
    other = nt(ip, z, EXACT)
    mixed = 0.5 * (cross[:, half:] + nt(z[:half], ip, EXACT))
    gram[:, 0:half] = basis[:half, :half]
    gram[:, half : 2 * half] = basis[:half, half:]
    gram[:, 2 * half : 3 * half] = basis[half:, half:]
    gram[:, 3 * half : 4 * half] = cross[:, :half]
    gram[:, 4 * half : 5 * half] = mixed
    gram[:, 5 * half : 6 * half] = other[:, half:]
    gram[:, 6 * half :] = jnp.zeros((half, LANE - 6 * half), F32)


def node_scales(f, both, span):
    shift = f[both + 1 : both + 2, span]
    return jnp.sqrt(safe(f[both : both + 1, span])), jnp.where(shift == 0.0, 1.0, shift)


def restrict_kernel(
    window_s, fc, fl, fh, ic, il, ih, col, gram, info, out, win, weighted, packed
):
    count, size = col.shape[1], col.shape[2]
    half = ic.shape[0]
    width = 2 * half
    for part, (f, img) in enumerate(((fl, il), (fc, ic), (fh, ih))):
        for b in range(count):
            span = slice(b * size, (b + 1) * size)
            root, shift = node_scales(f, width, span)
            field = jnp.concatenate([f[:half, span], img[:, span]], axis=0)
            smooth = field * (damping / shift)
            win[part * count + b] = smooth / root
            if part == 1:
                weighted[b * width : (b + 1) * width, :] = root * (
                    field - (1.0 + spectral_shift) * smooth
                )
    for b in range(count):
        acc = weighted[b * width : (b + 1) * width, :] + col[0, b : b + 1, :] * win[count + b]
        for s in range(3):
            acc = acc + col[1 + s, b : b + 1, :] * win[window_s[b, s]]
        weighted[b * width : (b + 1) * width, :] = acc
    sums = nt(jnp.ones((8, size), F32), weighted[...], EXACT)
    packed[...] = gram[...]
    for b in range(count):
        packed[b : b + 1, LANE - width :] = sums[0:1, b * width : (b + 1) * width]
        packed[count + b : count + b + 1, LANE - width :] = info[b : b + 1, 0:width]
    value = packed[...]
    for i in range(out.shape[0]):
        out[i] = value


def relay_kernel(got, out, packed):
    members, rows, _ = got.shape
    deep = members // GROUPS
    width = LANE // GROUPS
    total = got[0]
    for i in range(1, members):
        total = total + got[i]
    packed[0:rows, :] = total
    for i in range(members):
        g, j = i // deep, i % deep
        at = rows + j * rows
        packed[at : at + rows, g * width : (g + 1) * width] = got[i][:, LANE - width :]
    value = packed[...]
    for i in range(out.shape[0]):
        out[i] = value


def add_kernel(got, out):
    total = got[0]
    for i in range(1, got.shape[0]):
        total = total + got[i]
    for i in range(out.shape[0]):
        out[i] = total


def sum4(xs, ys):
    return (xs[0] * ys[0] + xs[1] * ys[1]) + (xs[2] * ys[2] + xs[3] * ys[3])


def inverse4(e):
    def g(i, j):
        return e[min(i, j), max(i, j)]

    def minor(r0, r1, c0, c1):
        return g(r0, c0) * g(r1, c1) - g(r0, c1) * g(r1, c0)

    s0, s1, s2 = minor(0, 1, 0, 1), minor(0, 1, 0, 2), minor(0, 1, 0, 3)
    s3, s4, s5 = minor(0, 1, 1, 2), minor(0, 1, 1, 3), minor(0, 1, 2, 3)
    c5, c4, c3 = minor(2, 3, 2, 3), minor(2, 3, 1, 3), minor(2, 3, 1, 2)
    c2, c1, c0 = minor(2, 3, 0, 3), minor(2, 3, 0, 2), minor(2, 3, 0, 1)
    r = 1.0 / (((s0 * c5 - s1 * c4) + (s2 * c3 + s3 * c2)) + (s5 * c0 - s4 * c1))
    q = {
        (0, 0): (g(1, 1) * c5 - g(1, 2) * c4 + g(1, 3) * c3) * r,
        (0, 1): (g(0, 2) * c4 - g(0, 1) * c5 - g(0, 3) * c3) * r,
        (0, 2): (g(3, 1) * s5 - g(3, 2) * s4 + g(3, 3) * s3) * r,
        (0, 3): (g(2, 2) * s4 - g(2, 1) * s5 - g(2, 3) * s3) * r,
        (1, 1): (g(0, 0) * c5 - g(0, 2) * c2 + g(0, 3) * c1) * r,
        (1, 2): (g(3, 2) * s2 - g(3, 0) * s5 - g(3, 3) * s1) * r,
        (1, 3): (g(2, 0) * s5 - g(2, 2) * s2 + g(2, 3) * s1) * r,
        (2, 2): (g(3, 0) * s4 - g(3, 1) * s2 + g(3, 3) * s0) * r,
        (2, 3): (g(2, 1) * s2 - g(2, 0) * s4 - g(2, 3) * s0) * r,
        (3, 3): (g(2, 0) * s3 - g(2, 1) * s1 + g(2, 2) * s0) * r,
    }
    return [[q[min(i, j), max(i, j)] for j in range(4)] for i in range(4)]


def inverse8(e):
    q = inverse4(e)
    side = [[e[i, 4 + j] for i in range(4)] for j in range(4)]
    w = [[sum4(q[i], side[j]) for j in range(4)] for i in range(4)]
    wt = [[w[i][j] for i in range(4)] for j in range(4)]
    schur = {
        (i, j): e[4 + i, 4 + j] - sum4(side[i], wt[j]) for i in range(4) for j in range(i, 4)
    }
    x = inverse4(schur)
    u = [[-sum4(w[i], x[j]) for j in range(4)] for i in range(4)]
    full = [[None] * 8 for _ in range(8)]
    for i in range(4):
        for j in range(4):
            full[4 + i][4 + j] = x[i][j]
            full[i][4 + j] = u[i][j]
            full[4 + j][i] = u[i][j]
            if j >= i:
                full[i][j] = q[i][j] - sum4(u[i], w[j])
                full[j][i] = full[i][j]
    return full


def inverse2(e):
    r = 1.0 / (e[0, 0] * e[1, 1] - e[0, 1] * e[0, 1])
    off = -e[0, 1] * r
    return [[e[1, 1] * r, off], [off, e[0, 0] * r]]


def spread_block(tile, k, width, shape):
    s = k % 8
    cols = [jnp.broadcast_to(tile[:, k + j : k + j + 1], shape) for j in range(width)]
    entries = {
        (i, j): jnp.broadcast_to(cols[j][s + i : s + i + 1, :], shape)
        for i in range(width)
        for j in range(i, width)
    }
    rows = [jnp.broadcast_to(tile[s + i : s + i + 1, :], shape) for i in range(width)]
    return cols, entries, rows


def invert_dense(matrix, width, block_inverse):
    n = matrix.shape[0]
    shape = (8, n)
    tiles = [matrix[8 * i : 8 * i + 8, :] for i in range(n // 8)]
    lane, sub = iota(shape, 1), iota(shape, 0)
    for k in range(0, n, width):
        at, s = k // 8, k % 8
        cols, entries, rows = spread_block(tiles[at], k, width, shape)
        inside = (lane >= k) & (lane < k + width)
        rows = [
            jnp.where(inside, jnp.where(lane == k + i, 1.0, 0.0), rows[i]) for i in range(width)
        ]
        q = block_inverse(entries)
        new = []
        for i in range(width):
            value = q[i][0] * rows[0]
            for j in range(1, width):
                value = value + q[i][j] * rows[j]
            new.append(value)
        for i in range(n // 8):
            old = tiles[i]
            value = jnp.where(inside, 0.0, old)
            if i != at or width < 8:
                for j in range(width):
                    c = cols[j] if i == at else jnp.broadcast_to(old[:, k + j : k + j + 1], shape)
                    value = value - c * new[j]
            if i == at:
                for j in range(width):
                    value = jnp.where(sub == s + j, new[j], value)
            tiles[i] = value
    return jnp.concatenate(tiles, axis=0)


def inverse_factor(matrix, unit):
    n = matrix.shape[0]
    shape = (8, 2 * n)
    work = jnp.concatenate([matrix, unit], axis=1)
    tiles = [work[8 * i : 8 * i + 8, :] for i in range(n // 8)]
    sub = iota(shape, 0)
    for k in range(0, n, 4):
        at, s = k // 8, k % 8
        cols, e, rows = spread_block(tiles[at], k, 4, shape)
        low, inv, new = {}, [], []
        for i in range(4):
            value, row = e[i, i], rows[i]
            for m in range(i):
                value = value - low[i, m] * low[i, m]
                row = row - low[i, m] * new[m]
            inv.append(1.0 / jnp.sqrt(value))
            new.append(row * inv[i])
            for j in range(i + 1, 4):
                value = e[i, j]
                for m in range(i):
                    value = value - low[i, m] * low[j, m]
                low[j, i] = value * inv[i]
        back = [None] * 4
        for i in (3, 2, 1, 0):
            value = new[i]
            for m in range(i + 1, 4):
                value = value - low[m, i] * back[m]
            back[i] = value * inv[i]
        for i in range(at, n // 8):
            old = tiles[i]
            value = old
            for j in range(4):
                c = cols[j] if i == at else jnp.broadcast_to(old[:, k + j : k + j + 1], shape)
                value = value - c * back[j]
            if i == at:
                value = jnp.where(sub >= s + 4, value, old)
                for j in range(4):
                    value = jnp.where(sub == s + j, new[j], value)
            tiles[i] = value
    return jnp.concatenate(tiles, axis=0)[:, n:]


def split3(value):
    high = value.astype(BF16)
    rest = value - high.astype(F32)
    mid = rest.astype(BF16)
    low = (rest - mid.astype(F32)).astype(BF16)
    return high, mid, low


def coarse_kernel(coarse_s, start_s, got, coef, gain, gram, uw, info, mat, hot, upper, pivots):
    members, depth, _ = got.shape
    rows = 16
    half = rows
    deep = (depth - rows) // rows
    width = LANE // GROUPS
    nc = mat.shape[0]
    count = coarse_s.shape[0]
    total = got[0, 0:rows]
    for y in range(1, members):
        total = total + got[y, 0:rows]
    gram[...] = total
    for y in range(members):
        for j in range(deep):
            at = (y * deep + j) * 8
            src = rows + j * rows
            uw[at : at + 8, :] = got[y, src : src + 8]
            info[at : at + 8, :] = got[y, src + 8 : src + 16]
    blocks = uw.shape[0]
    lanes = iota((blocks, nc), 1)
    agg = jnp.zeros((1, nc), F32)
    tiles = jnp.zeros((nc, nc), F32)
    for g in range(GROUPS):
        at = g * width
        values = [info[:, at + s : at + s + 1] for s in range(4)]
        ids = [info[:, at + 4 + s : at + 5 + s].astype(jnp.int32) for s in range(4)]
        here = lanes == ids[0]
        block_degree = values[0] + values[1] + values[2] + values[3]
        agg = agg + jnp.sum(jnp.where(here, block_degree, 0.0), axis=0, keepdims=True)
        spread = jnp.where(here, values[0], 0.0)
        for s in range(1, 4):
            spread = spread + jnp.where(lanes == ids[s], values[s], 0.0)
        member = jnp.where(here, 1.0, 0.0)
        hot[g] = member
        member = member.astype(BF16)
        for piece in split3(spread):
            tiles = tiles + tn(member, piece)
    same = iota((nc, nc), 0) == iota((nc, nc), 1)
    agg_col = jnp.sum(jnp.where(same, agg, 0.0), axis=1, keepdims=True)
    inv_row = 1.0 / jnp.sqrt(agg)
    inv_col = 1.0 / jnp.sqrt(agg_col)
    mat[...] = (jnp.where(same, (1.0 + spectral_shift) * agg, 0.0) - tiles) * inv_col * inv_row

    grams = total[:, 0:half]
    square = iota((half, half), 0) == iota((half, half), 1)
    diag_row = jnp.sum(jnp.where(square, grams, 0.0), axis=0, keepdims=True)
    diag_col = jnp.sum(jnp.where(square, grams, 0.0), axis=1, keepdims=True)
    unit_row, unit_col = 1.0 / jnp.sqrt(diag_row), 1.0 / jnp.sqrt(diag_col)
    inverse = invert_dense(grams * unit_row * unit_col, 2, inverse2) * unit_row * unit_col
    ritz = nn(total[:, 3 * half : 4 * half], inverse, EXACT)
    coef[...] = ritz
    combine = jnp.concatenate([-ritz, jnp.where(square, 1.0, 0.0)], axis=1)
    rhs = jnp.zeros((half, nc), F32)
    for g in range(GROUPS):
        block_rhs = nt(combine, uw[:, g * width : (g + 1) * width], EXACT)
        rhs = rhs + nn(block_rhs, hot[g], EXACT)
    rhs = rhs * inv_row

    block = min(LANE, nc)
    steps = nc // block

    def eliminate(step, _):
        at = pl.multiple_of(step * block, block)
        pivot = invert_dense(mat[pl.ds(at, block), pl.ds(at, block)], 8, inverse8)
        pivots[pl.ds(at, block), :] = pivot
        for j in range(steps - 1):

            @pl.when(step == j)
            def _():
                lo, hi = j * block, (j + 1) * block
                strip = nn(pivot, mat[lo:hi, hi:], EXACT)
                upper[lo:hi, hi:] = strip
                mat[hi:, hi:] = mat[hi:, hi:] - nn(mat[hi:, lo:hi], strip, EXACT)

        return 0

    lax.fori_loop(0, steps, eliminate, 0)
    for j in range(steps - 1):
        lo, hi = j * block, (j + 1) * block
        rest = rhs[:, hi:] - nn(rhs[:, lo:hi], upper[lo:hi, hi:], EXACT)
        rhs = jnp.concatenate([rhs[:, :hi], rest], axis=1)
    error = nn(rhs[:, nc - block :], pivots[nc - block :, :], EXACT)
    for j in reversed(range(steps - 1)):
        lo, hi = j * block, (j + 1) * block
        head = nn(rhs[:, lo:hi], pivots[lo:hi, :], EXACT) - nt(error, upper[lo:hi, hi:], EXACT)
        error = jnp.concatenate([head, error], axis=1)
    lifted = error * inv_row
    wide = iota((1, nc), 1)
    picks = []
    for j in range(24):
        at = jnp.clip(start_s[0] - 8 + j, 0, count - 1)
        picks.append(jnp.where(wide == coarse_s[at], 1.0, 0.0))
    picks.append(jnp.zeros((8, nc), F32))
    gain[...] = nt(lifted, jnp.concatenate(picks, axis=0), EXACT)


def correct_kernel(
    window_s, self_t, link_t, fc, fl, fh, ic, il, ih, coef, gain,
    residual, corrected, scaled, win, second,
):
    count, size = self_t.shape[0], self_t.shape[1]
    half = ic.shape[0]
    both = 2 * half
    ritz = coef[...]
    gains = gain[...]
    for part, (f, img) in enumerate(((fl, il), (fc, ic), (fh, ih))):
        res = img[...] - nn(ritz, f[:half, :], EXACT)
        if part == 1:
            residual[...] = res
        for b in range(count):
            span = slice(b * size, (b + 1) * size)
            root, shift = node_scales(f, both, span)
            j = part * count + b
            field = damping * res[:, span] / shift + root * gains[:, j : j + 1]
            win[j] = (field / root).astype(BF16)
            if part == 1:
                second[:, span] = field
    for b in range(count):
        span = slice(b * size, (b + 1) * size)
        root, shift = node_scales(fc, both, span)
        acc = apply_tiles(window_s, self_t, link_t, win, b, count)
        field = second[:, span]
        after = field - acc / root + spectral_shift * field
        field = field + damping * (residual[:, span] - after) / shift
        corrected[:, span] = field
        scaled[:, span] = (field / root).astype(BF16)


def search_kernel(window_s, self_t, link_t, w, sc, sl, sh, fc, ix, ip, out, win, image_w):
    count, size = self_t.shape[0], self_t.shape[1]
    half = w.shape[0]
    for part, s in enumerate((sl, sc, sh)):
        for b in range(count):
            win[part * count + b] = s[:, b * size : (b + 1) * size]
    for b in range(count):
        span = slice(b * size, (b + 1) * size)
        acc = apply_tiles(window_s, self_t, link_t, win, b, count)
        image_w[:, span] = w[:, span] - acc / jnp.sqrt(fc[2 * half : 2 * half + 1, span])
    field = w[...]
    field_image = image_w[...]
    zz = fc[: 2 * half, :]
    images = jnp.concatenate([ix[...], ip[...]], axis=0)
    value = jnp.concatenate(
        [
            nt(field, zz, EXACT),
            nt(field, field, EXACT),
            0.5 * (nt(field, images, EXACT) + nt(field_image, zz, EXACT)),
            nt(field, field_image, EXACT),
            jnp.zeros((half, LANE - 6 * half), F32),
        ],
        axis=1,
    )
    for i in range(out.shape[0]):
        out[i] = value


def project_kernel(got, gram, out):
    h = gram.shape[0]
    n = 3 * h
    new = got[0]
    for i in range(1, got.shape[0]):
        new = new + got[i]
    old = gram[...]
    zero = jnp.zeros((h, h), F32)
    unit = jnp.where(iota((n, n), 0) == iota((n, n), 1), 1.0, 0.0)

    def whole(xx, xp, pp, wx, ww, wp):
        upper = jnp.concatenate(
            [
                jnp.concatenate([0.5 * xx, zero, xp], axis=1),
                jnp.concatenate([wx, 0.5 * ww, wp], axis=1),
                jnp.concatenate([zero, zero, 0.5 * pp], axis=1),
            ],
            axis=0,
        )
        return upper + nt(unit, upper, EXACT)

    def piece(a, i):
        return a[:, i * h : (i + 1) * h]

    gram_b = whole(
        piece(old, 0), piece(old, 1), piece(old, 2), piece(new, 0), piece(new, 2), piece(new, 1)
    )
    gram_a = whole(
        piece(old, 3), piece(old, 4), piece(old, 5), piece(new, 3), piece(new, 5), piece(new, 4)
    )
    inverse = inverse_factor(gram_b, unit)
    out[...] = nt(nn(inverse, gram_a, EXACT), inverse, EXACT)


def body(self_tiles, link_tiles, links, coarse_row, vectors, directions):
    count, size = self_tiles.shape[0], self_tiles.shape[1]
    mine = vectors.shape[0]
    slab = count * size
    vec = lax.axis_size("vec")
    k = mine * vec
    row_axes = ("z", "y", "core")
    row_index = lax.axis_index(row_axes)
    row_count = lax.axis_size(row_axes)
    stage_one = ("z", "core")
    n_one = lax.axis_size(stage_one)
    n_two = lax.axis_size("y")
    forward = [(i, i + 1) for i in range(row_count - 1)]
    backward = [(i + 1, i) for i in range(row_count - 1)]

    def halo(a):
        return lax.ppermute(a, row_axes, forward), lax.ppermute(a, row_axes, backward)

    start = row_index * count
    start_s = start.reshape(1).astype(jnp.int32)
    links_s = lax.dynamic_slice_in_dim(links, start, count, 0)
    window_s = links_s - (start - count)

    both = jnp.broadcast_to(
        jnp.concatenate([vectors, directions], axis=0)[None], (vec, 2 * mine, slab)
    )
    both = lax.all_to_all(both, "vec", 0, 0)
    nodes, col, info = run(
        prep_kernel,
        (links_s, coarse_row, start_s, self_tiles, link_tiles),
        (arr((8, slab)), arr((4, count, size)), arr((count, LANE))),
        smem=3,
        work=1 << 30,
    )
    fc = run(pack_kernel, (both, nodes), arr((2 * k + 8, slab)))
    fl, fh = halo(fc)
    ic, ip, gram = run(
        image_kernel,
        (window_s, self_tiles, link_tiles, fc, fl, fh),
        (arr((k, slab)), arr((k, slab)), arr((k, LANE))),
        scratch=(pltpu.VMEM((3 * count, 2 * k, size), BF16),),
        smem=1,
    )
    il, ih = halo(ic)
    sent = run(
        restrict_kernel,
        (window_s, fc, fl, fh, ic, il, ih, col, gram, info),
        arr((n_one, 2 * count, LANE)),
        scratch=(
            pltpu.VMEM((3 * count, 2 * k, size), F32),
            pltpu.VMEM((count * 2 * k, size), F32),
            pltpu.VMEM((2 * count, LANE), F32),
        ),
        smem=1,
    )
    got = lax.all_to_all(sent, stage_one, 0, 0)
    depth = 2 * count * (1 + n_one // GROUPS)
    sent = run(
        relay_kernel,
        (got,),
        arr((n_two, depth, LANE)),
        scratch=(pltpu.VMEM((depth, LANE), F32),),
    )
    got = lax.all_to_all(sent, "y", 0, 0)
    coarse_count = coarse_row.shape[0] // 2
    blocks = n_two * (n_one // GROUPS) * count
    coef, gain, gram = run(
        coarse_kernel,
        (coarse_row, start_s, got),
        (arr((k, k)), arr((k, 32)), arr((k, LANE))),
        scratch=(
            pltpu.VMEM((blocks, LANE), F32),
            pltpu.VMEM((blocks, LANE), F32),
            pltpu.VMEM((coarse_count, coarse_count), F32),
            pltpu.VMEM((GROUPS, blocks, coarse_count), F32),
            pltpu.VMEM((coarse_count, coarse_count), F32),
            pltpu.VMEM((coarse_count, min(LANE, coarse_count)), F32),
        ),
        smem=2,
    )
    residual, corrected, scaled = run(
        correct_kernel,
        (window_s, self_tiles, link_tiles, fc, fl, fh, ic, il, ih, coef, gain),
        (arr((k, slab)), arr((k, slab)), arr((k, slab), BF16)),
        scratch=(pltpu.VMEM((3 * count, k, size), BF16), pltpu.VMEM((k, slab), F32)),
        smem=1,
    )
    sl, sh = halo(scaled)
    sent = run(
        search_kernel,
        (window_s, self_tiles, link_tiles, corrected, scaled, sl, sh, fc, ic, ip),
        arr((n_one, k, LANE)),
        scratch=(pltpu.VMEM((3 * count, k, size), BF16), pltpu.VMEM((k, slab), F32)),
        smem=1,
    )
    got = lax.all_to_all(sent, stage_one, 0, 0)
    sent = run(add_kernel, (got,), arr((n_two, k, LANE)))
    got = lax.all_to_all(sent, "y", 0, 0)
    projected = run(project_kernel, (got, gram), arr((3 * k, 3 * k)))
    at = lax.axis_index("vec") * mine
    return (
        lax.dynamic_slice_in_dim(residual, at, mine, 0),
        lax.dynamic_slice_in_dim(corrected, at, mine, 0),
        projected,
    )


def row_split(rows):
    return (8, rows // 16, 2) if rows >= 64 else (2, rows // 4, 2)


def solution(mesh):
    z, y, core = row_split(mesh.shape["rows"])
    split = Mesh(
        mesh.devices.reshape(z, y, core, mesh.shape["vec"]), ("z", "y", "core", "vec")
    )
    rows = ("z", "y", "core")
    in_specs = (
        P(rows, None, None),
        P(rows, None, None, None),
        P(),
        P(),
        P("vec", rows),
        P("vec", rows),
    )
    out_specs = (P("vec", rows), P("vec", rows), P())
    return jax.shard_map(body, mesh=split, in_specs=in_specs, out_specs=out_specs, check_vma=False)
```

```python
import jax
import jax.numpy as jnp
from jax import lax
from jax.experimental import pallas as pl
from jax.experimental.pallas import tpu as pltpu
from jax.sharding import Mesh, PartitionSpec as P

spectral_shift = 0.25
damping = 0.6
LANE = 128
GROUPS = 4

F32 = jnp.float32
BF16 = jnp.bfloat16
EXACT = lax.Precision.HIGHEST


def nn(left, right, precision=None):
    return lax.dot_general(
        left, right, (((1,), (0,)), ((), ())), precision=precision, preferred_element_type=F32
    )


def nt(left, right, precision=None):
    return lax.dot_general(
        left, right, (((1,), (1,)), ((), ())), precision=precision, preferred_element_type=F32
    )


def tn(left, right, precision=None):
    return lax.dot_general(
        left, right, (((0,), (0,)), ((), ())), precision=precision, preferred_element_type=F32
    )


def iota(shape, dim):
    return lax.broadcasted_iota(jnp.int32, shape, dim)


def run(kernel, inputs, outputs, scratch=(), smem=0, work=0):
    in_specs = [
        pl.BlockSpec(memory_space=pltpu.SMEM if i < smem else pltpu.VMEM)
        for i in range(len(inputs))
    ]
    single = not isinstance(outputs, (list, tuple))
    shapes = [outputs] if single else list(outputs)
    specs = [pl.BlockSpec(memory_space=pltpu.VMEM) for _ in shapes]
    return pl.pallas_call(
        kernel,
        in_specs=in_specs,
        out_specs=specs[0] if single else specs,
        out_shape=shapes[0] if single else shapes,
        scratch_shapes=list(scratch),
        compiler_params=pltpu.CompilerParams(vmem_limit_bytes=16 << 20),
        cost_estimate=pl.CostEstimate(
            flops=work, bytes_accessed=sum(a.size * a.dtype.itemsize for a in inputs), transcendentals=0
        ),
    )(*inputs)


def arr(shape, dtype=F32):
    return jax.ShapeDtypeStruct(shape, dtype)


def safe(value):
    return jnp.where(value > 0.0, value, 1.0)


def prep_kernel(links_s, coarse_s, start_s, self_t, link_t, nodes, col, info):
    count, size = self_t.shape[0], self_t.shape[1]
    ones = jnp.ones((8, size), BF16)
    diagonal = iota((size, size), 0) == iota((size, size), 1)
    lane = iota((1, LANE), 1)
    for b in range(count):
        own = self_t[b]
        degree = nt(ones, own)[0:1]
        col[0, b : b + 1, :] = degree
        row = jnp.where(lane == 0, jnp.sum(degree, axis=1, keepdims=True), 0.0)
        ids = jnp.where(lane == 4, coarse_s[start_s[0] + b], 0)
        for s in range(3):
            tile = link_t[b, s]
            part = nt(ones, tile)[0:1]
            degree = degree + part
            row = jnp.where(lane == 1 + s, jnp.sum(part, axis=1, keepdims=True), row)
            ids = jnp.where(lane == 5 + s, coarse_s[links_s[b, s]], ids)
            col[1 + s, b : b + 1, :] = jnp.sum(tile.astype(F32), axis=0, keepdims=True)
        diag = jnp.sum(jnp.where(diagonal, own.astype(F32), 0.0), axis=0, keepdims=True)
        span = slice(b * size, (b + 1) * size)
        nodes[0:1, span] = degree
        nodes[1:2, span] = 1.0 + spectral_shift - diag / degree
        info[b : b + 1, :] = row + ids.astype(F32)
    nodes[2:8, :] = jnp.zeros((6, nodes.shape[1]), F32)


def pack_kernel(both, nodes, out):
    members, twice, _ = both.shape
    mine = twice // 2
    for v in range(members):
        out[v * mine : (v + 1) * mine, :] = both[v, :mine]
        out[(members + v) * mine : (members + v + 1) * mine, :] = both[v, mine:]
    out[members * twice :, :] = nodes[...]


def apply_tiles(window_s, self_t, link_t, win, b, count):
    acc = nt(win[count + b], self_t[b])
    for s in range(3):
        acc = acc + nt(win[window_s[b, s]], link_t[b, s])
    return acc


def image_kernel(window_s, self_t, link_t, fc, fl, fh, image_x, image_p, gram, win):
    count, size = self_t.shape[0], self_t.shape[1]
    half = image_x.shape[0]
    both = 2 * half
    for part, f in enumerate((fl, fc, fh)):
        for b in range(count):
            span = slice(b * size, (b + 1) * size)
            root = jnp.sqrt(safe(f[both : both + 1, span]))
            win[part * count + b] = (f[:both, span] / root).astype(BF16)
    for b in range(count):
        acc = apply_tiles(window_s, self_t, link_t, win, b, count)
        span = slice(b * size, (b + 1) * size)
        value = fc[:both, span] - acc / jnp.sqrt(fc[both : both + 1, span])
        image_x[:, span] = value[:half]
        image_p[:, span] = value[half:]
    z = fc[:both, :]
    ix = image_x[...]
    ip = image_p[...]
    basis = nt(z, z, EXACT)
    cross = nt(ix, z, EXACT)
    other = nt(ip, z, EXACT)
    mixed = 0.5 * (cross[:, half:] + nt(z[:half], ip, EXACT))
    gram[:, 0:half] = basis[:half, :half]
    gram[:, half : 2 * half] = basis[:half, half:]
    gram[:, 2 * half : 3 * half] = basis[half:, half:]
    gram[:, 3 * half : 4 * half] = cross[:, :half]
    gram[:, 4 * half : 5 * half] = mixed
    gram[:, 5 * half : 6 * half] = other[:, half:]
    gram[:, 6 * half :] = jnp.zeros((half, LANE - 6 * half), F32)


def node_scales(f, both, span):
    shift = f[both + 1 : both + 2, span]
    return jnp.sqrt(safe(f[both : both + 1, span])), jnp.where(shift == 0.0, 1.0, shift)


def restrict_kernel(
    window_s, fc, fl, fh, ic, il, ih, col, gram, info, out, win, weighted, packed
):
    count, size = col.shape[1], col.shape[2]
    half = ic.shape[0]
    width = 2 * half
    for part, (f, img) in enumerate(((fl, il), (fc, ic), (fh, ih))):
        for b in range(count):
            span = slice(b * size, (b + 1) * size)
            root, shift = node_scales(f, width, span)
            field = jnp.concatenate([f[:half, span], img[:, span]], axis=0)
            smooth = field * (damping / shift)
            win[part * count + b] = smooth / root
            if part == 1:
                weighted[b * width : (b + 1) * width, :] = root * (
                    field - (1.0 + spectral_shift) * smooth
                )
    for b in range(count):
        acc = weighted[b * width : (b + 1) * width, :] + col[0, b : b + 1, :] * win[count + b]
        for s in range(3):
            acc = acc + col[1 + s, b : b + 1, :] * win[window_s[b, s]]
        weighted[b * width : (b + 1) * width, :] = acc
    sums = nt(jnp.ones((8, size), F32), weighted[...], EXACT)
    packed[...] = gram[...]
    for b in range(count):
        packed[b : b + 1, LANE - width :] = sums[0:1, b * width : (b + 1) * width]
        packed[count + b : count + b + 1, LANE - width :] = info[b : b + 1, 0:width]
    value = packed[...]
    for i in range(out.shape[0]):
        out[i] = value


def relay_kernel(got, out, packed):
    members, rows, _ = got.shape
    deep = members // GROUPS
    width = LANE // GROUPS
    total = got[0]
    for i in range(1, members):
        total = total + got[i]
    packed[0:rows, :] = total
    for i in range(members):
        g, j = i // deep, i % deep
        at = rows + j * rows
        packed[at : at + rows, g * width : (g + 1) * width] = got[i][:, LANE - width :]
    value = packed[...]
    for i in range(out.shape[0]):
        out[i] = value


def add_kernel(got, out):
    total = got[0]
    for i in range(1, got.shape[0]):
        total = total + got[i]
    for i in range(out.shape[0]):
        out[i] = total


def sum4(xs, ys):
    return (xs[0] * ys[0] + xs[1] * ys[1]) + (xs[2] * ys[2] + xs[3] * ys[3])


def inverse4(e):
    def g(i, j):
        return e[min(i, j), max(i, j)]

    def minor(r0, r1, c0, c1):
        return g(r0, c0) * g(r1, c1) - g(r0, c1) * g(r1, c0)

    s0, s1, s2 = minor(0, 1, 0, 1), minor(0, 1, 0, 2), minor(0, 1, 0, 3)
    s3, s4, s5 = minor(0, 1, 1, 2), minor(0, 1, 1, 3), minor(0, 1, 2, 3)
    c5, c4, c3 = minor(2, 3, 2, 3), minor(2, 3, 1, 3), minor(2, 3, 1, 2)
    c2, c1, c0 = minor(2, 3, 0, 3), minor(2, 3, 0, 2), minor(2, 3, 0, 1)
    r = 1.0 / (((s0 * c5 - s1 * c4) + (s2 * c3 + s3 * c2)) + (s5 * c0 - s4 * c1))
    q = {
        (0, 0): (g(1, 1) * c5 - g(1, 2) * c4 + g(1, 3) * c3) * r,
        (0, 1): (g(0, 2) * c4 - g(0, 1) * c5 - g(0, 3) * c3) * r,
        (0, 2): (g(3, 1) * s5 - g(3, 2) * s4 + g(3, 3) * s3) * r,
        (0, 3): (g(2, 2) * s4 - g(2, 1) * s5 - g(2, 3) * s3) * r,
        (1, 1): (g(0, 0) * c5 - g(0, 2) * c2 + g(0, 3) * c1) * r,
        (1, 2): (g(3, 2) * s2 - g(3, 0) * s5 - g(3, 3) * s1) * r,
        (1, 3): (g(2, 0) * s5 - g(2, 2) * s2 + g(2, 3) * s1) * r,
        (2, 2): (g(3, 0) * s4 - g(3, 1) * s2 + g(3, 3) * s0) * r,
        (2, 3): (g(2, 1) * s2 - g(2, 0) * s4 - g(2, 3) * s0) * r,
        (3, 3): (g(2, 0) * s3 - g(2, 1) * s1 + g(2, 2) * s0) * r,
    }
    return [[q[min(i, j), max(i, j)] for j in range(4)] for i in range(4)]


def inverse8(e):
    q = inverse4(e)
    side = [[e[i, 4 + j] for i in range(4)] for j in range(4)]
    w = [[sum4(q[i], side[j]) for j in range(4)] for i in range(4)]
    wt = [[w[i][j] for i in range(4)] for j in range(4)]
    schur = {
        (i, j): e[4 + i, 4 + j] - sum4(side[i], wt[j]) for i in range(4) for j in range(i, 4)
    }
    x = inverse4(schur)
    u = [[-sum4(w[i], x[j]) for j in range(4)] for i in range(4)]
    full = [[None] * 8 for _ in range(8)]
    for i in range(4):
        for j in range(4):
            full[4 + i][4 + j] = x[i][j]
            full[i][4 + j] = u[i][j]
            full[4 + j][i] = u[i][j]
            if j >= i:
                full[i][j] = q[i][j] - sum4(u[i], w[j])
                full[j][i] = full[i][j]
    return full


def inverse2(e):
    r = 1.0 / (e[0, 0] * e[1, 1] - e[0, 1] * e[0, 1])
    off = -e[0, 1] * r
    return [[e[1, 1] * r, off], [off, e[0, 0] * r]]


def spread_block(tile, k, width, shape):
    s = k % 8
    cols = [jnp.broadcast_to(tile[:, k + j : k + j + 1], shape) for j in range(width)]
    entries = {
        (i, j): jnp.broadcast_to(cols[j][s + i : s + i + 1, :], shape)
        for i in range(width)
        for j in range(i, width)
    }
    rows = [jnp.broadcast_to(tile[s + i : s + i + 1, :], shape) for i in range(width)]
    return cols, entries, rows


def invert_dense(matrix, width, block_inverse):
    n = matrix.shape[0]
    shape = (8, n)
    tiles = [matrix[8 * i : 8 * i + 8, :] for i in range(n // 8)]
    lane, sub = iota(shape, 1), iota(shape, 0)
    for k in range(0, n, width):
        at, s = k // 8, k % 8
        cols, entries, rows = spread_block(tiles[at], k, width, shape)
        inside = (lane >= k) & (lane < k + width)
        rows = [
            jnp.where(inside, jnp.where(lane == k + i, 1.0, 0.0), rows[i]) for i in range(width)
        ]
        q = block_inverse(entries)
        new = []
        for i in range(width):
            value = q[i][0] * rows[0]
            for j in range(1, width):
                value = value + q[i][j] * rows[j]
            new.append(value)
        for i in range(n // 8):
            old = tiles[i]
            value = jnp.where(inside, 0.0, old)
            if i != at or width < 8:
                for j in range(width):
                    c = cols[j] if i == at else jnp.broadcast_to(old[:, k + j : k + j + 1], shape)
                    value = value - c * new[j]
            if i == at:
                for j in range(width):
                    value = jnp.where(sub == s + j, new[j], value)
            tiles[i] = value
    return jnp.concatenate(tiles, axis=0)


def inverse_factor(matrix, unit):
    n = matrix.shape[0]
    shape = (8, 2 * n)
    work = jnp.concatenate([matrix, unit], axis=1)
    tiles = [work[8 * i : 8 * i + 8, :] for i in range(n // 8)]
    sub = iota(shape, 0)
    for k in range(0, n, 4):
        at, s = k // 8, k % 8
        cols, e, rows = spread_block(tiles[at], k, 4, shape)
        low, inv, new = {}, [], []
        for i in range(4):
            value, row = e[i, i], rows[i]
            for m in range(i):
                value = value - low[i, m] * low[i, m]
                row = row - low[i, m] * new[m]
            inv.append(1.0 / jnp.sqrt(value))
            new.append(row * inv[i])
            for j in range(i + 1, 4):
                value = e[i, j]
                for m in range(i):
                    value = value - low[i, m] * low[j, m]
                low[j, i] = value * inv[i]
        back = [None] * 4
        for i in (3, 2, 1, 0):
            value = new[i]
            for m in range(i + 1, 4):
                value = value - low[m, i] * back[m]
            back[i] = value * inv[i]
        for i in range(at, n // 8):
            old = tiles[i]
            value = old
            for j in range(4):
                c = cols[j] if i == at else jnp.broadcast_to(old[:, k + j : k + j + 1], shape)
                value = value - c * back[j]
            if i == at:
                value = jnp.where(sub >= s + 4, value, old)
                for j in range(4):
                    value = jnp.where(sub == s + j, new[j], value)
            tiles[i] = value
    return jnp.concatenate(tiles, axis=0)[:, n:]


def split3(value):
    high = value.astype(BF16)
    rest = value - high.astype(F32)
    mid = rest.astype(BF16)
    low = (rest - mid.astype(F32)).astype(BF16)
    return high, mid, low


def coarse_kernel(coarse_s, start_s, got, coef, gain, gram, uw, info, mat, hot, upper, pivots):
    members, depth, _ = got.shape
    rows = 16
    half = rows
    deep = (depth - rows) // rows
    width = LANE // GROUPS
    nc = mat.shape[0]
    count = coarse_s.shape[0]
    total = got[0, 0:rows]
    for y in range(1, members):
        total = total + got[y, 0:rows]
    gram[...] = total
    for y in range(members):
        for j in range(deep):
            at = (y * deep + j) * 8
            src = rows + j * rows
            uw[at : at + 8, :] = got[y, src : src + 8]
            info[at : at + 8, :] = got[y, src + 8 : src + 16]
    blocks = uw.shape[0]
    lanes = iota((blocks, nc), 1)
    agg = jnp.zeros((1, nc), F32)
    tiles = jnp.zeros((nc, nc), F32)
    for g in range(GROUPS):
        at = g * width
        values = [info[:, at + s : at + s + 1] for s in range(4)]
        ids = [info[:, at + 4 + s : at + 5 + s].astype(jnp.int32) for s in range(4)]
        here = lanes == ids[0]
        block_degree = values[0] + values[1] + values[2] + values[3]
        agg = agg + jnp.sum(jnp.where(here, block_degree, 0.0), axis=0, keepdims=True)
        spread = jnp.where(here, values[0], 0.0)
        for s in range(1, 4):
            spread = spread + jnp.where(lanes == ids[s], values[s], 0.0)
        member = jnp.where(here, 1.0, 0.0)
        hot[g] = member
        member = member.astype(BF16)
        for piece in split3(spread):
            tiles = tiles + tn(member, piece)
    same = iota((nc, nc), 0) == iota((nc, nc), 1)
    agg_col = jnp.sum(jnp.where(same, agg, 0.0), axis=1, keepdims=True)
    inv_row = 1.0 / jnp.sqrt(agg)
    inv_col = 1.0 / jnp.sqrt(agg_col)
    mat[...] = (jnp.where(same, (1.0 + spectral_shift) * agg, 0.0) - tiles) * inv_col * inv_row

    grams = total[:, 0:half]
    square = iota((half, half), 0) == iota((half, half), 1)
    diag_row = jnp.sum(jnp.where(square, grams, 0.0), axis=0, keepdims=True)
    diag_col = jnp.sum(jnp.where(square, grams, 0.0), axis=1, keepdims=True)
    unit_row, unit_col = 1.0 / jnp.sqrt(diag_row), 1.0 / jnp.sqrt(diag_col)
    inverse = invert_dense(grams * unit_row * unit_col, 2, inverse2) * unit_row * unit_col
    ritz = nn(total[:, 3 * half : 4 * half], inverse, EXACT)
    coef[...] = ritz
    combine = jnp.concatenate([-ritz, jnp.where(square, 1.0, 0.0)], axis=1)
    rhs = jnp.zeros((half, nc), F32)
    for g in range(GROUPS):
        block_rhs = nt(combine, uw[:, g * width : (g + 1) * width], EXACT)
        rhs = rhs + nn(block_rhs, hot[g], EXACT)
    rhs = rhs * inv_row

    block = min(LANE, nc)
    steps = nc // block

    def eliminate(step, _):
        at = pl.multiple_of(step * block, block)
        pivot = invert_dense(mat[pl.ds(at, block), pl.ds(at, block)], 8, inverse8)
        pivots[pl.ds(at, block), :] = pivot
        for j in range(steps - 1):

            @pl.when(step == j)
            def _():
                lo, hi = j * block, (j + 1) * block
                strip = nn(pivot, mat[lo:hi, hi:], EXACT)
                upper[lo:hi, hi:] = strip
                mat[hi:, hi:] = mat[hi:, hi:] - nn(mat[hi:, lo:hi], strip, EXACT)

        return 0

    lax.fori_loop(0, steps, eliminate, 0)
    for j in range(steps - 1):
        lo, hi = j * block, (j + 1) * block
        rest = rhs[:, hi:] - nn(rhs[:, lo:hi], upper[lo:hi, hi:], EXACT)
        rhs = jnp.concatenate([rhs[:, :hi], rest], axis=1)
    error = nn(rhs[:, nc - block :], pivots[nc - block :, :], EXACT)
    for j in reversed(range(steps - 1)):
        lo, hi = j * block, (j + 1) * block
        head = nn(rhs[:, lo:hi], pivots[lo:hi, :], EXACT) - nt(error, upper[lo:hi, hi:], EXACT)
        error = jnp.concatenate([head, error], axis=1)
    lifted = error * inv_row
    wide = iota((1, nc), 1)
    picks = []
    for j in range(24):
        at = jnp.clip(start_s[0] - 8 + j, 0, count - 1)
        picks.append(jnp.where(wide == coarse_s[at], 1.0, 0.0))
    picks.append(jnp.zeros((8, nc), F32))
    gain[...] = nt(lifted, jnp.concatenate(picks, axis=0), EXACT)


def correct_kernel(
    window_s, start_s, self_t, link_t, fc, fl, fh, ic, il, ih, coef, gain,
    my_residual, my_corrected, corrected, scaled, win, second, residual,
):
    count, size = self_t.shape[0], self_t.shape[1]
    half = ic.shape[0]
    both = 2 * half
    ritz = coef[...]
    gains = gain[...]
    for part, (f, img) in enumerate(((fl, il), (fc, ic), (fh, ih))):
        res = img[...] - nn(ritz, f[:half, :], EXACT)
        if part == 1:
            residual[...] = res
        for b in range(count):
            span = slice(b * size, (b + 1) * size)
            root, shift = node_scales(f, both, span)
            j = part * count + b
            field = damping * res[:, span] / shift + root * gains[:, j : j + 1]
            win[j] = (field / root).astype(BF16)
            if part == 1:
                second[:, span] = field
    for b in range(count):
        span = slice(b * size, (b + 1) * size)
        root, shift = node_scales(fc, both, span)
        acc = apply_tiles(window_s, self_t, link_t, win, b, count)
        field = second[:, span]
        after = field - acc / root + spectral_shift * field
        field = field + damping * (residual[:, span] - after) / shift
        corrected[:, span] = field
        scaled[:, span] = (field / root).astype(BF16)
    mine = my_residual.shape[0]
    pick = iota((mine, half), 1) == iota((mine, half), 0) + start_s[1] * mine
    pick = jnp.where(pick, 1.0, 0.0)
    my_residual[...] = nn(pick, residual[...], EXACT)
    my_corrected[...] = nn(pick, corrected[...], EXACT)


def search_kernel(window_s, self_t, link_t, w, sc, sl, sh, fc, ix, ip, out, win, image_w):
    count, size = self_t.shape[0], self_t.shape[1]
    half = w.shape[0]
    for part, s in enumerate((sl, sc, sh)):
        for b in range(count):
            win[part * count + b] = s[:, b * size : (b + 1) * size]
    for b in range(count):
        span = slice(b * size, (b + 1) * size)
        acc = apply_tiles(window_s, self_t, link_t, win, b, count)
        image_w[:, span] = w[:, span] - acc / jnp.sqrt(fc[2 * half : 2 * half + 1, span])
    field = w[...]
    field_image = image_w[...]
    zz = fc[: 2 * half, :]
    images = jnp.concatenate([ix[...], ip[...]], axis=0)
    value = jnp.concatenate(
        [
            nt(field, zz, EXACT),
            nt(field, field, EXACT),
            0.5 * (nt(field, images, EXACT) + nt(field_image, zz, EXACT)),
            nt(field, field_image, EXACT),
            jnp.zeros((half, LANE - 6 * half), F32),
        ],
        axis=1,
    )
    for i in range(out.shape[0]):
        out[i] = value


def project_kernel(got, gram, out):
    h = gram.shape[0]
    n = 3 * h
    new = got[0]
    for i in range(1, got.shape[0]):
        new = new + got[i]
    old = gram[...]
    zero = jnp.zeros((h, h), F32)
    unit = jnp.where(iota((n, n), 0) == iota((n, n), 1), 1.0, 0.0)

    def whole(xx, xp, pp, wx, ww, wp):
        upper = jnp.concatenate(
            [
                jnp.concatenate([0.5 * xx, zero, xp], axis=1),
                jnp.concatenate([wx, 0.5 * ww, wp], axis=1),
                jnp.concatenate([zero, zero, 0.5 * pp], axis=1),
            ],
            axis=0,
        )
        return upper + nt(unit, upper, EXACT)

    def piece(a, i):
        return a[:, i * h : (i + 1) * h]

    gram_b = whole(
        piece(old, 0), piece(old, 1), piece(old, 2), piece(new, 0), piece(new, 2), piece(new, 1)
    )
    gram_a = whole(
        piece(old, 3), piece(old, 4), piece(old, 5), piece(new, 3), piece(new, 5), piece(new, 4)
    )
    inverse = inverse_factor(gram_b, unit)
    out[...] = nt(nn(inverse, gram_a, EXACT), inverse, EXACT)


def body(self_tiles, link_tiles, links, coarse_row, vectors, directions):
    count, size = self_tiles.shape[0], self_tiles.shape[1]
    mine = vectors.shape[0]
    slab = count * size
    vec = lax.axis_size("vec")
    k = mine * vec
    row_axes = ("z", "y", "core")
    row_index = lax.axis_index(row_axes)
    row_count = lax.axis_size(row_axes)
    stage_one = ("z", "core")
    n_one = lax.axis_size(stage_one)
    n_two = lax.axis_size("y")
    forward = [(i, i + 1) for i in range(row_count - 1)]
    backward = [(i + 1, i) for i in range(row_count - 1)]

    def halo(a):
        return lax.ppermute(a, row_axes, forward), lax.ppermute(a, row_axes, backward)

    start = row_index * count
    start_s = jnp.stack([start, lax.axis_index("vec")]).astype(jnp.int32)
    links_s = lax.dynamic_slice_in_dim(links, start, count, 0)
    window_s = links_s - (start - count)

    both = jnp.broadcast_to(
        jnp.concatenate([vectors, directions], axis=0)[None], (vec, 2 * mine, slab)
    )
    both = lax.all_to_all(both, "vec", 0, 0)
    nodes, col, info = run(
        prep_kernel,
        (links_s, coarse_row, start_s, self_tiles, link_tiles),
        (arr((8, slab)), arr((4, count, size)), arr((count, LANE))),
        smem=3,
        work=1 << 30,
    )
    fc = run(pack_kernel, (both, nodes), arr((2 * k + 8, slab)))
    fl, fh = halo(fc)
    ic, ip, gram = run(
        image_kernel,
        (window_s, self_tiles, link_tiles, fc, fl, fh),
        (arr((k, slab)), arr((k, slab)), arr((k, LANE))),
        scratch=(pltpu.VMEM((3 * count, 2 * k, size), BF16),),
        smem=1,
    )
    il, ih = halo(ic)
    sent = run(
        restrict_kernel,
        (window_s, fc, fl, fh, ic, il, ih, col, gram, info),
        arr((n_one, 2 * count, LANE)),
        scratch=(
            pltpu.VMEM((3 * count, 2 * k, size), F32),
            pltpu.VMEM((count * 2 * k, size), F32),
            pltpu.VMEM((2 * count, LANE), F32),
        ),
        smem=1,
    )
    got = lax.all_to_all(sent, stage_one, 0, 0)
    depth = 2 * count * (1 + n_one // GROUPS)
    sent = run(
        relay_kernel,
        (got,),
        arr((n_two, depth, LANE)),
        scratch=(pltpu.VMEM((depth, LANE), F32),),
    )
    got = lax.all_to_all(sent, "y", 0, 0)
    coarse_count = coarse_row.shape[0] // 2
    blocks = n_two * (n_one // GROUPS) * count
    coef, gain, gram = run(
        coarse_kernel,
        (coarse_row, start_s, got),
        (arr((k, k)), arr((k, 32)), arr((k, LANE))),
        scratch=(
            pltpu.VMEM((blocks, LANE), F32),
            pltpu.VMEM((blocks, LANE), F32),
            pltpu.VMEM((coarse_count, coarse_count), F32),
            pltpu.VMEM((GROUPS, blocks, coarse_count), F32),
            pltpu.VMEM((coarse_count, coarse_count), F32),
            pltpu.VMEM((coarse_count, min(LANE, coarse_count)), F32),
        ),
        smem=2,
    )
    residual, my_corrected, corrected, scaled = run(
        correct_kernel,
        (window_s, start_s, self_tiles, link_tiles, fc, fl, fh, ic, il, ih, coef, gain),
        (arr((mine, slab)), arr((mine, slab)), arr((k, slab)), arr((k, slab), BF16)),
        scratch=(
            pltpu.VMEM((3 * count, k, size), BF16),
            pltpu.VMEM((k, slab), F32),
            pltpu.VMEM((k, slab), F32),
        ),
        smem=2,
    )
    sl, sh = halo(scaled)
    sent = run(
        search_kernel,
        (window_s, self_tiles, link_tiles, corrected, scaled, sl, sh, fc, ic, ip),
        arr((n_one, k, LANE)),
        scratch=(pltpu.VMEM((3 * count, k, size), BF16), pltpu.VMEM((k, slab), F32)),
        smem=1,
    )
    got = lax.all_to_all(sent, stage_one, 0, 0)
    sent = run(add_kernel, (got,), arr((n_two, k, LANE)))
    got = lax.all_to_all(sent, "y", 0, 0)
    projected = run(project_kernel, (got, gram), arr((3 * k, 3 * k)))
    return residual, my_corrected, projected


def row_split(rows):
    return (8, rows // 16, 2) if rows >= 64 else (2, rows // 4, 2)


def solution(mesh):
    z, y, core = row_split(mesh.shape["rows"])
    split = Mesh(
        mesh.devices.reshape(z, y, core, mesh.shape["vec"]), ("z", "y", "core", "vec")
    )
    rows = ("z", "y", "core")
    in_specs = (
        P(rows, None, None),
        P(rows, None, None, None),
        P(),
        P(),
        P("vec", rows),
        P("vec", rows),
    )
    out_specs = (P("vec", rows), P("vec", rows), P())
    return jax.shard_map(body, mesh=split, in_specs=in_specs, out_specs=out_specs, check_vma=False)
```

```python
import functools
import jax
import jax.numpy as jnp
from jax import lax
from jax.experimental import pallas as pl
from jax.experimental.pallas import tpu as pltpu
from jax.sharding import Mesh, PartitionSpec as P

spectral_shift = 0.25
damping = 0.6
LANE = 128
GROUPS = 4

F32 = jnp.float32
BF16 = jnp.bfloat16
EXACT = lax.Precision.HIGHEST


def nn(left, right, precision=None):
    return lax.dot_general(
        left, right, (((1,), (0,)), ((), ())), precision=precision, preferred_element_type=F32
    )


def nt(left, right, precision=None):
    return lax.dot_general(
        left, right, (((1,), (1,)), ((), ())), precision=precision, preferred_element_type=F32
    )


def tn(left, right, precision=None):
    return lax.dot_general(
        left, right, (((0,), (0,)), ((), ())), precision=precision, preferred_element_type=F32
    )


def iota(shape, dim):
    return lax.broadcasted_iota(jnp.int32, shape, dim)


def run(kernel, inputs, outputs, scratch=(), smem=0):
    in_specs = [
        pl.BlockSpec(memory_space=pltpu.SMEM if i < smem else pltpu.VMEM)
        for i in range(len(inputs))
    ]
    single = not isinstance(outputs, (list, tuple))
    shapes = [outputs] if single else list(outputs)
    specs = [pl.BlockSpec(memory_space=pltpu.VMEM) for _ in shapes]
    return pl.pallas_call(
        kernel,
        in_specs=in_specs,
        out_specs=specs[0] if single else specs,
        out_shape=shapes[0] if single else shapes,
        scratch_shapes=list(scratch),
        compiler_params=pltpu.CompilerParams(vmem_limit_bytes=16 << 20),
    )(*inputs)


def arr(shape, dtype=F32):
    return jax.ShapeDtypeStruct(shape, dtype)


def safe(value):
    return jnp.where(value > 0.0, value, 1.0)


def stack_kernel(vectors, directions, out):
    mine = vectors.shape[0]
    for v in range(out.shape[0]):
        out[v, :mine] = vectors[...]
        out[v, mine:] = directions[...]


def prep_kernel(links_s, coarse_s, start_s, self_t, link_t, both, fields, col, info):
    count, size = self_t.shape[0], self_t.shape[1]
    members, twice, _ = both.shape
    mine = twice // 2
    base = members * twice
    for v in range(members):
        fields[v * mine : (v + 1) * mine, :] = both[v, :mine]
        fields[(members + v) * mine : (members + v + 1) * mine, :] = both[v, mine:]
    ones = jnp.ones((8, size), BF16)
    diagonal = iota((size, size), 0) == iota((size, size), 1)
    lane = iota((1, LANE), 1)
    for b in range(count):
        own = self_t[b]
        degree = nt(ones, own)[0:1]
        col[0, b : b + 1, :] = degree
        row = jnp.where(lane == 0, jnp.sum(degree, axis=1, keepdims=True), 0.0)
        ids = jnp.where(lane == 4, coarse_s[start_s[0] + b], 0)
        for s in range(3):
            tile = link_t[b, s]
            part = nt(ones, tile)[0:1]
            degree = degree + part
            row = jnp.where(lane == 1 + s, jnp.sum(part, axis=1, keepdims=True), row)
            ids = jnp.where(lane == 5 + s, coarse_s[links_s[s, start_s[0] + b]], ids)
            col[1 + s, b : b + 1, :] = jnp.sum(tile.astype(F32), axis=0, keepdims=True)
        diag = jnp.sum(jnp.where(diagonal, own.astype(F32), 0.0), axis=0, keepdims=True)
        span = slice(b * size, (b + 1) * size)
        fields[base : base + 1, span] = degree
        fields[base + 1 : base + 2, span] = 1.0 + spectral_shift - diag / degree
        info[b : b + 1, :] = row + ids.astype(F32)
    fields[base + 2 : base + 8, :] = jnp.zeros((6, fields.shape[1]), F32)


def linked(links_s, start_s, b, s, count):
    return links_s[s, start_s[0] + b] - start_s[0] + count


def apply_tiles(links_s, start_s, self_t, link_t, win, b, count):
    acc = nt(win[count + b], self_t[b])
    for s in range(3):
        acc = acc + nt(win[linked(links_s, start_s, b, s, count)], link_t[b, s])
    return acc


def image_kernel(links_s, start_s, self_t, link_t, fc, fl, fh, image_x, image_p, gram, win):
    count, size = self_t.shape[0], self_t.shape[1]
    half = image_x.shape[0]
    both = 2 * half
    for part, f in enumerate((fl, fc, fh)):
        for b in range(count):
            span = slice(b * size, (b + 1) * size)
            root = jnp.sqrt(safe(f[both : both + 1, span]))
            win[part * count + b] = (f[:both, span] / root).astype(BF16)
    for b in range(count):
        acc = apply_tiles(links_s, start_s, self_t, link_t, win, b, count)
        span = slice(b * size, (b + 1) * size)
        value = fc[:both, span] - acc / jnp.sqrt(fc[both : both + 1, span])
        image_x[:, span] = value[:half]
        image_p[:, span] = value[half:]
    z = fc[:both, :]
    ix = image_x[...]
    ip = image_p[...]
    basis = nt(z, z, EXACT)
    cross = nt(ix, z, EXACT)
    other = nt(ip, z, EXACT)
    mixed = 0.5 * (cross[:, half:] + nt(z[:half], ip, EXACT))
    gram[:, 0:half] = basis[:half, :half]
    gram[:, half : 2 * half] = basis[:half, half:]
    gram[:, 2 * half : 3 * half] = basis[half:, half:]
    gram[:, 3 * half : 4 * half] = cross[:, :half]
    gram[:, 4 * half : 5 * half] = mixed
    gram[:, 5 * half : 6 * half] = other[:, half:]
    gram[:, 6 * half :] = jnp.zeros((half, LANE - 6 * half), F32)


def node_scales(f, both, span):
    shift = f[both + 1 : both + 2, span]
    return jnp.sqrt(safe(f[both : both + 1, span])), jnp.where(shift == 0.0, 1.0, shift)


def restrict_kernel(
    links_s, start_s, fc, fl, fh, ic, il, ih, col, gram, info, out, win, weighted, packed
):
    count, size = col.shape[1], col.shape[2]
    half = ic.shape[0]
    width = 2 * half
    for part, (f, img) in enumerate(((fl, il), (fc, ic), (fh, ih))):
        for b in range(count):
            span = slice(b * size, (b + 1) * size)
            root, shift = node_scales(f, width, span)
            field = jnp.concatenate([f[:half, span], img[:, span]], axis=0)
            smooth = field * (damping / shift)
            win[part * count + b] = smooth / root
            if part == 1:
                weighted[b * width : (b + 1) * width, :] = root * (
                    field - (1.0 + spectral_shift) * smooth
                )
    for b in range(count):
        acc = weighted[b * width : (b + 1) * width, :] + col[0, b : b + 1, :] * win[count + b]
        for s in range(3):
            acc = acc + col[1 + s, b : b + 1, :] * win[linked(links_s, start_s, b, s, count)]
        weighted[b * width : (b + 1) * width, :] = acc
    sums = nt(jnp.ones((8, size), F32), weighted[...], EXACT)
    packed[...] = gram[...]
    for b in range(count):
        packed[b : b + 1, LANE - width :] = sums[0:1, b * width : (b + 1) * width]
        packed[count + b : count + b + 1, LANE - width :] = info[b : b + 1, 0:width]
    value = packed[...]
    for i in range(out.shape[0]):
        out[i] = value


def relay_kernel(got, out, packed):
    members, rows, _ = got.shape
    half = rows // 2
    deep = members // GROUPS
    width = LANE // GROUPS
    total = got[0]
    for i in range(1, members):
        total = total + got[i]
    packed[0:rows, :] = total
    tail = rows + deep * half
    if members * 8 < LANE:
        packed[tail : tail + half, :] = jnp.zeros((half, LANE), F32)
    for i in range(members):
        g, j = i // deep, i % deep
        at = rows + j * half
        mine = got[i]
        packed[at : at + half, g * width : (g + 1) * width] = mine[:half, LANE - width :]
        packed[tail : tail + half, i * 8 : (i + 1) * 8] = mine[half:, LANE - width : LANE - width + 8]
    value = packed[...]
    for i in range(out.shape[0]):
        out[i] = value


def add_kernel(got, out):
    total = got[0]
    for i in range(1, got.shape[0]):
        total = total + got[i]
    for i in range(out.shape[0]):
        out[i] = total


def lane_copy(tile, at):
    return jnp.broadcast_to(tile[:, at : at + 1], tile.shape)


def row_copy(tile, at):
    return jnp.broadcast_to(tile[at : at + 1, :], tile.shape)


def solve_tile(cols, tile, more, sub):
    fields = list(cols) + [tile] + list(more)
    final = tile
    for p in range(0, 8, 2):
        q = p + 1
        vp, vq = fields[p], fields[q]
        a, c = row_copy(vp, p), row_copy(vp, q)
        b, d = row_copy(vq, p), row_copy(vq, q)
        det = a * d - b * c
        r = 1.0 / det
        ar, br, cr, dr = a * r, b * r, c * r, d * r
        f0, f1 = vp * dr - vq * cr, vq * ar - vp * br
        f0 = jnp.where(sub == p, 1.0 - dr, jnp.where(sub == q, cr, f0))
        f1 = jnp.where(sub == p, br, jnp.where(sub == q, 1.0 - ar, f1))
        x0, x1 = row_copy(fields[8], p), row_copy(fields[8], q)
        root = 1.0 / jnp.sqrt(a)
        final = jnp.where(sub == p, x0 * root, final)
        final = jnp.where(sub == q, (x1 * a - c * x0) * (root / jnp.sqrt(det)), final)
        for m in range(q + 1, len(fields)):
            x = fields[m]
            fields[m] = x - (f0 * row_copy(x, p) + f1 * row_copy(x, q))
    return fields[8], final, fields[9:]


def sum8(terms):
    a, b, c, d, e, f, g, h = terms
    return ((a + b) + (c + d)) + ((e + f) + (g + h))


def invert_dense(matrix, whole):
    n = matrix.shape[0]
    shape = (8, n)
    tiles = [matrix[8 * i : 8 * i + 8, :] for i in range(n // 8)]
    lane, sub = iota(shape, 1), iota(shape, 0)
    cols = [lane_copy(tiles[0], j) for j in range(8)]
    for at in range(n // 8):
        k = 8 * at
        last = at + 1 == n // 8
        inside = (lane >= k) & (lane < k + 8)
        start = jnp.where(inside, jnp.where(lane == sub + k, 1.0, 0.0), tiles[at])
        ahead = [] if last else [lane_copy(tiles[at], k + 8 + j) for j in range(8)]
        new, final, ahead = solve_tile(cols, start, ahead, sub)
        rows = [row_copy(new, j) for j in range(8)]
        for i in range(0 if whole else at + 1, n // 8):
            if i != at:
                old = tiles[i]
                parts = [lane_copy(old, k + j) for j in range(8)]
                if i == at + 1:
                    cols = [
                        lane_copy(old, k + 8 + j)
                        - sum8([parts[m] * row_copy(ahead[j], m) for m in range(8)])
                        for j in range(8)
                    ]
                tiles[i] = jnp.where(inside, 0.0, old) - sum8(
                    [parts[j] * rows[j] for j in range(8)]
                )
        tiles[at] = new if whole else jnp.where(lane <= sub + k, final, 0.0)
    return jnp.concatenate(tiles, axis=0)


def unit_scales(matrix):
    square = iota(matrix.shape, 0) == iota(matrix.shape, 1)
    diag = jnp.where(square, matrix, 0.0)
    row = 1.0 / jnp.sqrt(jnp.sum(diag, axis=0, keepdims=True))
    return row, 1.0 / jnp.sqrt(jnp.sum(diag, axis=1, keepdims=True))


def split3(value):
    high = value.astype(BF16)
    rest = value - high.astype(F32)
    mid = rest.astype(BF16)
    low = (rest - mid.astype(F32)).astype(BF16)
    return high, mid, low


def coarse_kernel(coarse_s, start_s, got, coef, gain, gram, uw, info, mat, hot, upper, pivots):
    members, depth, _ = got.shape
    rows = 16
    half = rows
    deep = (depth - rows) // 8 - 1
    width = LANE // GROUPS
    nc = mat.shape[0]
    count = coarse_s.shape[0]
    total = got[0, 0:rows]
    for y in range(1, members):
        total = total + got[y, 0:rows]
    gram[...] = total
    for y in range(members):
        for j in range(deep):
            at = (y * deep + j) * 8
            src = rows + j * 8
            uw[at : at + 8, :] = got[y, src : src + 8]
            for g in range(GROUPS):
                i = (g * deep + j) * 8
                info[at : at + 8, g * width : g * width + 8] = got[y, depth - 8 :, i : i + 8]
    blocks = uw.shape[0]
    lanes = iota((blocks, nc), 1)
    agg = jnp.zeros((1, nc), F32)
    tiles = jnp.zeros((nc, nc), F32)
    for g in range(GROUPS):
        at = g * width
        values = [info[:, at + s : at + s + 1] for s in range(4)]
        ids = [info[:, at + 4 + s : at + 5 + s].astype(jnp.int32) for s in range(4)]
        here = lanes == ids[0]
        block_degree = values[0] + values[1] + values[2] + values[3]
        agg = agg + jnp.sum(jnp.where(here, block_degree, 0.0), axis=0, keepdims=True)
        spread = jnp.where(here, values[0], 0.0)
        for s in range(1, 4):
            spread = spread + jnp.where(lanes == ids[s], values[s], 0.0)
        member = jnp.where(here, 1.0, 0.0)
        hot[g] = member
        member = member.astype(BF16)
        for piece in split3(spread):
            tiles = tiles + tn(member, piece)
    same = iota((nc, nc), 0) == iota((nc, nc), 1)
    agg_col = jnp.sum(jnp.where(same, agg, 0.0), axis=1, keepdims=True)
    inv_row = 1.0 / jnp.sqrt(agg)
    inv_col = 1.0 / jnp.sqrt(agg_col)
    mat[...] = (jnp.where(same, (1.0 + spectral_shift) * agg, 0.0) - tiles) * inv_col * inv_row

    grams = total[:, 0:half]
    square = iota((half, half), 0) == iota((half, half), 1)
    unit_row, unit_col = unit_scales(grams)
    inverse = invert_dense(grams * unit_row * unit_col, True) * unit_row * unit_col
    ritz = nn(total[:, 3 * half : 4 * half], inverse, EXACT)
    coef[...] = ritz
    combine = jnp.concatenate([-ritz, jnp.where(square, 1.0, 0.0)], axis=1)
    rhs = jnp.zeros((half, nc), F32)
    for g in range(GROUPS):
        block_rhs = nt(combine, uw[:, g * width : (g + 1) * width], EXACT)
        rhs = rhs + nn(block_rhs, hot[g], EXACT)
    rhs = rhs * inv_row

    block = min(LANE, nc)
    steps = nc // block

    def eliminate(step, _):
        at = pl.multiple_of(step * block, block)
        pivot = invert_dense(mat[pl.ds(at, block), pl.ds(at, block)], False)
        pivots[pl.ds(at, block), :] = pivot
        for j in range(steps - 1):

            @pl.when(step == j)
            def _():
                lo, hi = j * block, (j + 1) * block
                strip = nn(pivot, mat[lo:hi, hi:], EXACT)
                upper[lo:hi, hi:] = strip
                mat[hi:, hi:] = mat[hi:, hi:] - tn(strip, strip, EXACT)

        return 0

    lax.fori_loop(0, steps, eliminate, 0)
    halves = []
    for j in range(steps):
        lo, hi = j * block, (j + 1) * block
        head = nt(rhs[:, :block], pivots[lo:hi, :], EXACT)
        halves.append(head)
        if hi < nc:
            rhs = rhs[:, block:] - nn(head, upper[lo:hi, hi:], EXACT)
    error = nn(halves[-1], pivots[nc - block :, :], EXACT)
    for j in reversed(range(steps - 1)):
        lo, hi = j * block, (j + 1) * block
        head = halves[j] - nt(error, upper[lo:hi, hi:], EXACT)
        error = jnp.concatenate([nn(head, pivots[lo:hi, :], EXACT), error], axis=1)
    lifted = error * inv_row
    wide = iota((1, nc), 1)
    picks = []
    for j in range(24):
        at = jnp.clip(start_s[0] - 8 + j, 0, count - 1)
        picks.append(jnp.where(wide == coarse_s[at], 1.0, 0.0))
    picks.append(jnp.zeros((8, nc), F32))
    gain[...] = nt(lifted, jnp.concatenate(picks, axis=0), EXACT)


def correct_kernel(
    links_s, start_s, self_t, link_t, fc, fl, fh, ic, il, ih, coef, gain,
    my_residual, my_corrected, corrected, scaled, win, second, residual,
):
    count, size = self_t.shape[0], self_t.shape[1]
    half = ic.shape[0]
    both = 2 * half
    ritz = coef[...]
    gains = gain[...]
    for part, (f, img) in enumerate(((fl, il), (fc, ic), (fh, ih))):
        res = img[...] - nn(ritz, f[:half, :], EXACT)
        if part == 1:
            residual[...] = res
        for b in range(count):
            span = slice(b * size, (b + 1) * size)
            root, shift = node_scales(f, both, span)
            j = part * count + b
            field = damping * res[:, span] / shift + root * gains[:, j : j + 1]
            win[j] = (field / root).astype(BF16)
            if part == 1:
                second[:, span] = field
    for b in range(count):
        span = slice(b * size, (b + 1) * size)
        root, shift = node_scales(fc, both, span)
        acc = apply_tiles(links_s, start_s, self_t, link_t, win, b, count)
        field = second[:, span]
        after = field - acc / root + spectral_shift * field
        field = field + damping * (residual[:, span] - after) / shift
        corrected[:, span] = field
        scaled[:, span] = (field / root).astype(BF16)
    mine = my_residual.shape[0]
    pick = iota((mine, half), 1) == iota((mine, half), 0) + start_s[1] * mine
    pick = jnp.where(pick, 1.0, 0.0)
    my_residual[...] = nn(pick, residual[...], EXACT)
    my_corrected[...] = nn(pick, corrected[...], EXACT)


def search_kernel(links_s, start_s, self_t, link_t, w, sc, sl, sh, fc, ix, ip, out, win, image_w):
    count, size = self_t.shape[0], self_t.shape[1]
    half = w.shape[0]
    for part, s in enumerate((sl, sc, sh)):
        for b in range(count):
            win[part * count + b] = s[:, b * size : (b + 1) * size]
    for b in range(count):
        span = slice(b * size, (b + 1) * size)
        acc = apply_tiles(links_s, start_s, self_t, link_t, win, b, count)
        image_w[:, span] = w[:, span] - acc / jnp.sqrt(fc[2 * half : 2 * half + 1, span])
    field = w[...]
    field_image = image_w[...]
    zz = fc[: 2 * half, :]
    images = jnp.concatenate([ix[...], ip[...]], axis=0)
    value = jnp.concatenate(
        [
            nt(field, zz, EXACT),
            nt(field, field, EXACT),
            0.5 * (nt(field, images, EXACT) + nt(field_image, zz, EXACT)),
            nt(field, field_image, EXACT),
            jnp.zeros((half, LANE - 6 * half), F32),
        ],
        axis=1,
    )
    for i in range(out.shape[0]):
        out[i] = value


def project_kernel(got, gram, out):
    h = gram.shape[0]
    n = 3 * h
    new = got[0]
    for i in range(1, got.shape[0]):
        new = new + got[i]
    old = gram[...]
    zero = jnp.zeros((h, h), F32)
    unit = jnp.where(iota((n, n), 0) == iota((n, n), 1), 1.0, 0.0)

    def whole(xx, xp, pp, wx, ww, wp):
        upper = jnp.concatenate(
            [
                jnp.concatenate([0.5 * xx, zero, xp], axis=1),
                jnp.concatenate([wx, 0.5 * ww, wp], axis=1),
                jnp.concatenate([zero, zero, 0.5 * pp], axis=1),
            ],
            axis=0,
        )
        return upper + nt(unit, upper, EXACT)

    def piece(a, i):
        return a[:, i * h : (i + 1) * h]

    gram_b = whole(
        piece(old, 0), piece(old, 1), piece(old, 2), piece(new, 0), piece(new, 2), piece(new, 1)
    )
    gram_a = whole(
        piece(old, 3), piece(old, 4), piece(old, 5), piece(new, 3), piece(new, 5), piece(new, 4)
    )
    unit_row, unit_col = unit_scales(gram_b)
    inverse = invert_dense(gram_b * unit_row * unit_col, False) * unit_row
    out[...] = nt(nn(inverse, gram_a, EXACT), inverse, EXACT)


def body(self_tiles, link_tiles, links, coarse_row, vectors, directions):
    count, size = self_tiles.shape[0], self_tiles.shape[1]
    mine = vectors.shape[0]
    slab = count * size
    vec = lax.axis_size("vec")
    k = mine * vec
    row_axes = ("z", "y", "core")
    row_index = lax.axis_index(row_axes)
    row_count = lax.axis_size(row_axes)
    stage_one = ("z", "core")
    n_one = lax.axis_size(stage_one)
    n_two = lax.axis_size("y")
    forward = [(i, i + 1) for i in range(row_count - 1)]
    backward = [(i + 1, i) for i in range(row_count - 1)]

    def halo(a):
        return lax.ppermute(a, row_axes, forward), lax.ppermute(a, row_axes, backward)

    start_s = jnp.stack([row_index * count, lax.axis_index("vec")]).astype(jnp.int32)
    links_s = links.T
    both = run(stack_kernel, (vectors, directions), arr((vec, 2 * mine, slab)))
    both, start_s = lax.optimization_barrier((both, start_s))
    both = lax.all_to_all(both, "vec", 0, 0)
    fc, col, info = run(
        prep_kernel,
        (links_s, coarse_row, start_s, self_tiles, link_tiles, both),
        (arr((2 * k + 8, slab)), arr((4, count, size)), arr((count, LANE))),
        smem=3,
    )
    fl, fh = halo(fc)
    ic, ip, gram = run(
        image_kernel,
        (links_s, start_s, self_tiles, link_tiles, fc, fl, fh),
        (arr((k, slab)), arr((k, slab)), arr((k, LANE))),
        scratch=(pltpu.VMEM((3 * count, 2 * k, size), BF16),),
        smem=2,
    )
    il, ih = halo(ic)
    sent = run(
        restrict_kernel,
        (links_s, start_s, fc, fl, fh, ic, il, ih, col, gram, info),
        arr((n_one, 2 * count, LANE)),
        scratch=(
            pltpu.VMEM((3 * count, 2 * k, size), F32),
            pltpu.VMEM((count * 2 * k, size), F32),
            pltpu.VMEM((2 * count, LANE), F32),
        ),
        smem=2,
    )
    got = lax.all_to_all(sent, stage_one, 0, 0)
    depth = count * (3 + n_one // GROUPS)
    sent = run(
        relay_kernel,
        (got,),
        arr((n_two, depth, LANE)),
        scratch=(pltpu.VMEM((depth, LANE), F32),),
    )
    got = lax.all_to_all(sent, "y", 0, 0)
    coarse_count = coarse_row.shape[0] // 2
    blocks = n_two * (n_one // GROUPS) * count
    coef, gain, gram = run(
        coarse_kernel,
        (coarse_row, start_s, got),
        (arr((k, k)), arr((k, 32)), arr((k, LANE))),
        scratch=(
            pltpu.VMEM((blocks, LANE), F32),
            pltpu.VMEM((blocks, LANE), F32),
            pltpu.VMEM((coarse_count, coarse_count), F32),
            pltpu.VMEM((GROUPS, blocks, coarse_count), F32),
            pltpu.VMEM((coarse_count, coarse_count), F32),
            pltpu.VMEM((coarse_count, min(LANE, coarse_count)), F32),
        ),
        smem=2,
    )
    residual, my_corrected, corrected, scaled = run(
        correct_kernel,
        (links_s, start_s, self_tiles, link_tiles, fc, fl, fh, ic, il, ih, coef, gain),
        (arr((mine, slab)), arr((mine, slab)), arr((k, slab)), arr((k, slab), BF16)),
        scratch=(
            pltpu.VMEM((3 * count, k, size), BF16),
            pltpu.VMEM((k, slab), F32),
            pltpu.VMEM((k, slab), F32),
        ),
        smem=2,
    )
    sl, sh = halo(scaled)
    sent = run(
        search_kernel,
        (links_s, start_s, self_tiles, link_tiles, corrected, scaled, sl, sh, fc, ic, ip),
        arr((n_one, k, LANE)),
        scratch=(pltpu.VMEM((3 * count, k, size), BF16), pltpu.VMEM((k, slab), F32)),
        smem=2,
    )
    got = lax.all_to_all(sent, stage_one, 0, 0)
    sent = run(add_kernel, (got,), arr((n_two, k, LANE)))
    got = lax.all_to_all(sent, "y", 0, 0)
    projected = run(project_kernel, (got, gram), arr((3 * k, 3 * k)))
    return residual, my_corrected, projected


def row_split(rows):
    return (8, rows // 16, 2) if rows >= 64 else (2, rows // 4, 2)


def solution(mesh):
    z, y, core = row_split(mesh.shape["rows"])
    split = Mesh(
        mesh.devices.reshape(z, y, core, mesh.shape["vec"]), ("z", "y", "core", "vec")
    )
    rows = ("z", "y", "core")
    in_specs = (
        P(rows, None, None),
        P(rows, None, None, None),
        P(),
        P(),
        P("vec", rows),
        P("vec", rows),
    )
    out_specs = (P("vec", rows), P("vec", rows), P())
    return jax.shard_map(body, mesh=split, in_specs=in_specs, out_specs=out_specs, check_vma=False)
```

```python
import functools
import jax
import jax.numpy as jnp
from jax import lax
from jax.experimental import pallas as pl
from jax.experimental.pallas import tpu as pltpu
from jax.sharding import Mesh, PartitionSpec as P

spectral_shift = 0.25
damping = 0.6
LANE = 128
GROUPS = 4

F32 = jnp.float32
BF16 = jnp.bfloat16
EXACT = lax.Precision.HIGHEST


def nn(left, right, precision=None):
    return lax.dot_general(
        left, right, (((1,), (0,)), ((), ())), precision=precision, preferred_element_type=F32
    )


def nt(left, right, precision=None):
    return lax.dot_general(
        left, right, (((1,), (1,)), ((), ())), precision=precision, preferred_element_type=F32
    )


def tn(left, right, precision=None):
    return lax.dot_general(
        left, right, (((0,), (0,)), ((), ())), precision=precision, preferred_element_type=F32
    )


def iota(shape, dim):
    return lax.broadcasted_iota(jnp.int32, shape, dim)


def run(kernel, inputs, outputs, scratch=(), smem=0, hbm=()):
    in_specs = [
        pl.BlockSpec(
            memory_space=pltpu.SMEM if i < smem else pltpu.HBM if i in hbm else pltpu.VMEM
        )
        for i in range(len(inputs))
    ]
    single = not isinstance(outputs, (list, tuple))
    shapes = [outputs] if single else list(outputs)
    specs = [pl.BlockSpec(memory_space=pltpu.VMEM) for _ in shapes]
    return pl.pallas_call(
        kernel,
        in_specs=in_specs,
        out_specs=specs[0] if single else specs,
        out_shape=shapes[0] if single else shapes,
        scratch_shapes=list(scratch),
        compiler_params=pltpu.CompilerParams(vmem_limit_bytes=16 << 20),
    )(*inputs)


def arr(shape, dtype=F32):
    return jax.ShapeDtypeStruct(shape, dtype)


def safe(value):
    return jnp.where(value > 0.0, value, 1.0)


def stack_kernel(vectors, directions, out):
    mine = vectors.shape[0]
    for v in range(out.shape[0]):
        out[v, :mine] = vectors[...]
        out[v, mine:] = directions[...]


def prep_kernel(
    links_s, coarse_s, start_s, self_far, link_far, nodes, col, info, link_t, self_t, arrived
):
    count, size = self_t.shape[0], self_t.shape[1]
    copies = []
    for b in range(count):
        copies.append(pltpu.make_async_copy(self_far.at[b], self_t.at[b], arrived.at[b]))
        copies.append(pltpu.make_async_copy(link_far.at[b], link_t.at[b], arrived.at[count + b]))
    for copy in copies:
        copy.start()
    ones = jnp.ones((8, size), BF16)
    diagonal = iota((size, size), 0) == iota((size, size), 1)
    lane = iota((1, LANE), 1)
    for b in range(count):
        copies[2 * b].wait()
        copies[2 * b + 1].wait()
        own = self_t[b]
        degree = nt(ones, own)[0:1]
        col[0, b : b + 1, :] = degree
        row = jnp.where(lane == 0, jnp.sum(degree, axis=1, keepdims=True), 0.0)
        ids = jnp.where(lane == 4, coarse_s[start_s[0] + b], 0)
        for s in range(3):
            tile = link_t[b, s]
            part = nt(ones, tile)[0:1]
            degree = degree + part
            row = jnp.where(lane == 1 + s, jnp.sum(part, axis=1, keepdims=True), row)
            ids = jnp.where(lane == 5 + s, coarse_s[links_s[s, start_s[0] + b]], ids)
            col[1 + s, b : b + 1, :] = jnp.sum(tile.astype(F32), axis=0, keepdims=True)
        diag = jnp.sum(jnp.where(diagonal, own.astype(F32), 0.0), axis=0, keepdims=True)
        span = slice(b * size, (b + 1) * size)
        nodes[0:1, span] = degree
        nodes[1:2, span] = 1.0 + spectral_shift - diag / degree
        info[b : b + 1, :] = row + ids.astype(F32)
    nodes[2:8, :] = jnp.zeros((6, nodes.shape[1]), F32)


def pack_kernel(both, nodes, out):
    members, twice, _ = both.shape
    mine = twice // 2
    for v in range(members):
        out[v * mine : (v + 1) * mine, :] = both[v, :mine]
        out[(members + v) * mine : (members + v + 1) * mine, :] = both[v, mine:]
    out[members * twice :, :] = nodes[...]


def linked(links_s, start_s, b, s, count):
    return links_s[s, start_s[0] + b] - start_s[0] + count


def apply_tiles(links_s, start_s, self_t, link_t, win, b, count):
    acc = nt(win[count + b], self_t[b])
    for s in range(3):
        acc = acc + nt(win[linked(links_s, start_s, b, s, count)], link_t[b, s])
    return acc


def image_kernel(
    links_s, start_s, self_far, link_t, fc, fl, fh, image_x, image_p, gram, win, self_t, arrived
):
    count, size = self_t.shape[0], self_t.shape[1]
    copy = pltpu.make_async_copy(self_far, self_t, arrived)
    copy.start()
    half = image_x.shape[0]
    both = 2 * half
    for part, f in enumerate((fl, fc, fh)):
        for b in range(count):
            span = slice(b * size, (b + 1) * size)
            root = jnp.sqrt(safe(f[both : both + 1, span]))
            win[part * count + b] = (f[:both, span] / root).astype(BF16)
    copy.wait()
    for b in range(count):
        acc = apply_tiles(links_s, start_s, self_t, link_t, win, b, count)
        span = slice(b * size, (b + 1) * size)
        value = fc[:both, span] - acc / jnp.sqrt(fc[both : both + 1, span])
        image_x[:, span] = value[:half]
        image_p[:, span] = value[half:]
    z = fc[:both, :]
    ix = image_x[...]
    ip = image_p[...]
    basis = nt(z, z, EXACT)
    cross = nt(ix, z, EXACT)
    other = nt(ip, z, EXACT)
    mixed = 0.5 * (cross[:, half:] + nt(z[:half], ip, EXACT))
    gram[:, 0:half] = basis[:half, :half]
    gram[:, half : 2 * half] = basis[:half, half:]
    gram[:, 2 * half : 3 * half] = basis[half:, half:]
    gram[:, 3 * half : 4 * half] = cross[:, :half]
    gram[:, 4 * half : 5 * half] = mixed
    gram[:, 5 * half : 6 * half] = other[:, half:]
    gram[:, 6 * half :] = jnp.zeros((half, LANE - 6 * half), F32)


def node_scales(f, both, span):
    shift = f[both + 1 : both + 2, span]
    return jnp.sqrt(safe(f[both : both + 1, span])), jnp.where(shift == 0.0, 1.0, shift)


def restrict_kernel(
    links_s, start_s, fc, fl, fh, ic, il, ih, col, gram, info, out, win, weighted, packed
):
    count, size = col.shape[1], col.shape[2]
    half = ic.shape[0]
    width = 2 * half
    for part, (f, img) in enumerate(((fl, il), (fc, ic), (fh, ih))):
        for b in range(count):
            span = slice(b * size, (b + 1) * size)
            root, shift = node_scales(f, width, span)
            field = jnp.concatenate([f[:half, span], img[:, span]], axis=0)
            smooth = field * (damping / shift)
            win[part * count + b] = smooth / root
            if part == 1:
                weighted[b * width : (b + 1) * width, :] = root * (
                    field - (1.0 + spectral_shift) * smooth
                )
    for b in range(count):
        acc = weighted[b * width : (b + 1) * width, :] + col[0, b : b + 1, :] * win[count + b]
        for s in range(3):
            acc = acc + col[1 + s, b : b + 1, :] * win[linked(links_s, start_s, b, s, count)]
        weighted[b * width : (b + 1) * width, :] = acc
    sums = nt(jnp.ones((8, size), F32), weighted[...], EXACT)
    packed[...] = gram[...]
    for b in range(count):
        packed[b : b + 1, LANE - width :] = sums[0:1, b * width : (b + 1) * width]
        packed[count + b : count + b + 1, LANE - width :] = info[b : b + 1, 0:width]
    value = packed[...]
    for i in range(out.shape[0]):
        out[i] = value


def relay_kernel(got, out, packed):
    members, rows, _ = got.shape
    half = rows // 2
    deep = members // GROUPS
    width = LANE // GROUPS
    total = got[0]
    for i in range(1, members):
        total = total + got[i]
    packed[0:rows, :] = total
    tail = rows + deep * half
    if members * 8 < LANE:
        packed[tail : tail + half, :] = jnp.zeros((half, LANE), F32)
    for i in range(members):
        g, j = i // deep, i % deep
        at = rows + j * half
        mine = got[i]
        packed[at : at + half, g * width : (g + 1) * width] = mine[:half, LANE - width :]
        packed[tail : tail + half, i * 8 : (i + 1) * 8] = mine[half:, LANE - width : LANE - width + 8]
    value = packed[...]
    for i in range(out.shape[0]):
        out[i] = value


def add_kernel(got, out):
    total = got[0]
    for i in range(1, got.shape[0]):
        total = total + got[i]
    for i in range(out.shape[0]):
        out[i] = total


def lane_copy(tile, at):
    return jnp.broadcast_to(tile[:, at : at + 1], tile.shape)


def row_copy(tile, at):
    return jnp.broadcast_to(tile[at : at + 1, :], tile.shape)


def solve_tile(cols, tile, more, sub):
    fields = list(cols) + [tile] + list(more)
    final = tile
    for p in range(0, 8, 2):
        q = p + 1
        vp, vq = fields[p], fields[q]
        a, c = row_copy(vp, p), row_copy(vp, q)
        b, d = row_copy(vq, p), row_copy(vq, q)
        det = a * d - b * c
        r = 1.0 / det
        ar, br, cr, dr = a * r, b * r, c * r, d * r
        f0, f1 = vp * dr - vq * cr, vq * ar - vp * br
        f0 = jnp.where(sub == p, 1.0 - dr, jnp.where(sub == q, cr, f0))
        f1 = jnp.where(sub == p, br, jnp.where(sub == q, 1.0 - ar, f1))
        x0, x1 = row_copy(fields[8], p), row_copy(fields[8], q)
        root = 1.0 / jnp.sqrt(a)
        final = jnp.where(sub == p, x0 * root, final)
        final = jnp.where(sub == q, (x1 * a - c * x0) * (root / jnp.sqrt(det)), final)
        for m in range(q + 1, len(fields)):
            x = fields[m]
            fields[m] = x - (f0 * row_copy(x, p) + f1 * row_copy(x, q))
    return fields[8], final, fields[9:]


def sum8(terms):
    a, b, c, d, e, f, g, h = terms
    return ((a + b) + (c + d)) + ((e + f) + (g + h))


def invert_dense(matrix, whole):
    n = matrix.shape[0]
    shape = (8, n)
    tiles = [matrix[8 * i : 8 * i + 8, :] for i in range(n // 8)]
    lane, sub = iota(shape, 1), iota(shape, 0)
    cols = [lane_copy(tiles[0], j) for j in range(8)]
    for at in range(n // 8):
        k = 8 * at
        last = at + 1 == n // 8
        inside = (lane >= k) & (lane < k + 8)
        start = jnp.where(inside, jnp.where(lane == sub + k, 1.0, 0.0), tiles[at])
        ahead = [] if last else [lane_copy(tiles[at], k + 8 + j) for j in range(8)]
        new, final, ahead = solve_tile(cols, start, ahead, sub)
        rows = [row_copy(new, j) for j in range(8)]
        for i in range(0 if whole else at + 1, n // 8):
            if i != at:
                old = tiles[i]
                parts = [lane_copy(old, k + j) for j in range(8)]
                if i == at + 1:
                    cols = [
                        lane_copy(old, k + 8 + j)
                        - sum8([parts[m] * row_copy(ahead[j], m) for m in range(8)])
                        for j in range(8)
                    ]
                tiles[i] = jnp.where(inside, 0.0, old) - sum8(
                    [parts[j] * rows[j] for j in range(8)]
                )
        tiles[at] = new if whole else jnp.where(lane <= sub + k, final, 0.0)
    return jnp.concatenate(tiles, axis=0)


def unit_scales(matrix):
    square = iota(matrix.shape, 0) == iota(matrix.shape, 1)
    diag = jnp.where(square, matrix, 0.0)
    row = 1.0 / jnp.sqrt(jnp.sum(diag, axis=0, keepdims=True))
    return row, 1.0 / jnp.sqrt(jnp.sum(diag, axis=1, keepdims=True))


def split3(value):
    high = value.astype(BF16)
    rest = value - high.astype(F32)
    mid = rest.astype(BF16)
    low = (rest - mid.astype(F32)).astype(BF16)
    return high, mid, low


def coarse_kernel(coarse_s, start_s, got, coef, gain, gram, uw, info, mat, hot, upper, pivots):
    members, depth, _ = got.shape
    rows = 16
    half = rows
    deep = (depth - rows) // 8 - 1
    width = LANE // GROUPS
    nc = mat.shape[0]
    count = coarse_s.shape[0]
    total = got[0, 0:rows]
    for y in range(1, members):
        total = total + got[y, 0:rows]
    gram[...] = total
    for y in range(members):
        for j in range(deep):
            at = (y * deep + j) * 8
            src = rows + j * 8
            uw[at : at + 8, :] = got[y, src : src + 8]
            for g in range(GROUPS):
                i = (g * deep + j) * 8
                info[at : at + 8, g * width : g * width + 8] = got[y, depth - 8 :, i : i + 8]
    blocks = uw.shape[0]
    lanes = iota((blocks, nc), 1)
    agg = jnp.zeros((1, nc), F32)
    tiles = jnp.zeros((nc, nc), F32)
    for g in range(GROUPS):
        at = g * width
        values = [info[:, at + s : at + s + 1] for s in range(4)]
        ids = [info[:, at + 4 + s : at + 5 + s].astype(jnp.int32) for s in range(4)]
        here = lanes == ids[0]
        block_degree = values[0] + values[1] + values[2] + values[3]
        agg = agg + jnp.sum(jnp.where(here, block_degree, 0.0), axis=0, keepdims=True)
        spread = jnp.where(here, values[0], 0.0)
        for s in range(1, 4):
            spread = spread + jnp.where(lanes == ids[s], values[s], 0.0)
        member = jnp.where(here, 1.0, 0.0).astype(BF16)
        hot[g] = member
        pieces = tn(member, jnp.concatenate(split3(spread), axis=1))
        tiles = tiles + (pieces[:, :nc] + (pieces[:, nc : 2 * nc] + pieces[:, 2 * nc :]))
    same = iota((nc, nc), 0) == iota((nc, nc), 1)
    agg_col = jnp.sum(jnp.where(same, agg, 0.0), axis=1, keepdims=True)
    inv_row = 1.0 / jnp.sqrt(agg)
    inv_col = 1.0 / jnp.sqrt(agg_col)
    mat[...] = (jnp.where(same, (1.0 + spectral_shift) * agg, 0.0) - tiles) * inv_col * inv_row

    grams = total[:, 0:half]
    square = iota((half, half), 0) == iota((half, half), 1)
    unit_row, unit_col = unit_scales(grams)
    inverse = invert_dense(grams * unit_row * unit_col, True) * unit_row * unit_col
    ritz = nn(total[:, 3 * half : 4 * half], inverse, EXACT)
    coef[...] = ritz
    combine = jnp.concatenate([-ritz, jnp.where(square, 1.0, 0.0)], axis=1)
    rhs = jnp.zeros((half, nc), F32)
    for g in range(GROUPS):
        block_rhs = nt(combine, uw[:, g * width : (g + 1) * width], EXACT)
        pieces = nn(jnp.concatenate(split3(block_rhs), axis=0), hot[g])
        rhs = rhs + (pieces[:half] + (pieces[half : 2 * half] + pieces[2 * half :]))
    rhs = rhs * inv_row

    block = min(LANE, nc)
    steps = nc // block

    def eliminate(step, _):
        at = pl.multiple_of(step * block, block)
        pivot = invert_dense(mat[pl.ds(at, block), pl.ds(at, block)], False)
        pivots[pl.ds(at, block), :] = pivot
        for j in range(steps - 1):

            @pl.when(step == j)
            def _():
                lo, hi = j * block, (j + 1) * block
                strip = nn(pivot, mat[lo:hi, hi:], EXACT)
                upper[lo:hi, hi:] = strip
                mat[hi:, hi:] = mat[hi:, hi:] - tn(strip, strip, EXACT)

        return 0

    lax.fori_loop(0, steps, eliminate, 0)
    halves = []
    for j in range(steps):
        lo, hi = j * block, (j + 1) * block
        head = nt(rhs[:, :block], pivots[lo:hi, :], EXACT)
        halves.append(head)
        if hi < nc:
            rhs = rhs[:, block:] - nn(head, upper[lo:hi, hi:], EXACT)
    error = nn(halves[-1], pivots[nc - block :, :], EXACT)
    for j in reversed(range(steps - 1)):
        lo, hi = j * block, (j + 1) * block
        head = halves[j] - nt(error, upper[lo:hi, hi:], EXACT)
        error = jnp.concatenate([nn(head, pivots[lo:hi, :], EXACT), error], axis=1)
    lifted = error * inv_row
    wide = iota((1, nc), 1)
    picks = []
    for j in range(24):
        at = jnp.clip(start_s[0] - 8 + j, 0, count - 1)
        picks.append(jnp.where(wide == coarse_s[at], 1.0, 0.0))
    picks.append(jnp.zeros((8, nc), F32))
    gain[...] = nt(lifted, jnp.concatenate(picks, axis=0), EXACT)


def correct_kernel(
    links_s, start_s, self_t, link_t, fc, fl, fh, ic, il, ih, coef, gain,
    my_residual, my_corrected, corrected, scaled, win, second, residual,
):
    count, size = self_t.shape[0], self_t.shape[1]
    half = ic.shape[0]
    both = 2 * half
    ritz = coef[...]
    gains = gain[...]
    for part, (f, img) in enumerate(((fl, il), (fc, ic), (fh, ih))):
        res = img[...] - nn(ritz, f[:half, :], EXACT)
        if part == 1:
            residual[...] = res
        for b in range(count):
            span = slice(b * size, (b + 1) * size)
            root, shift = node_scales(f, both, span)
            j = part * count + b
            field = damping * res[:, span] / shift + root * gains[:, j : j + 1]
            win[j] = (field / root).astype(BF16)
            if part == 1:
                second[:, span] = field
    for b in range(count):
        span = slice(b * size, (b + 1) * size)
        root, shift = node_scales(fc, both, span)
        acc = apply_tiles(links_s, start_s, self_t, link_t, win, b, count)
        field = second[:, span]
        after = field - acc / root + spectral_shift * field
        field = field + damping * (residual[:, span] - after) / shift
        corrected[:, span] = field
        scaled[:, span] = (field / root).astype(BF16)
    mine = my_residual.shape[0]
    pick = iota((mine, half), 1) == iota((mine, half), 0) + start_s[1] * mine
    pick = jnp.where(pick, 1.0, 0.0)
    my_residual[...] = nn(pick, residual[...], EXACT)
    my_corrected[...] = nn(pick, corrected[...], EXACT)


def search_kernel(links_s, start_s, self_t, link_t, w, sc, sl, sh, fc, ix, ip, out, win, image_w):
    count, size = self_t.shape[0], self_t.shape[1]
    half = w.shape[0]
    for part, s in enumerate((sl, sc, sh)):
        for b in range(count):
            win[part * count + b] = s[:, b * size : (b + 1) * size]
    for b in range(count):
        span = slice(b * size, (b + 1) * size)
        acc = apply_tiles(links_s, start_s, self_t, link_t, win, b, count)
        image_w[:, span] = w[:, span] - acc / jnp.sqrt(fc[2 * half : 2 * half + 1, span])
    field = w[...]
    field_image = image_w[...]
    zz = fc[: 2 * half, :]
    images = jnp.concatenate([ix[...], ip[...]], axis=0)
    value = jnp.concatenate(
        [
            nt(field, zz, EXACT),
            nt(field, field, EXACT),
            0.5 * (nt(field, images, EXACT) + nt(field_image, zz, EXACT)),
            nt(field, field_image, EXACT),
            jnp.zeros((half, LANE - 6 * half), F32),
        ],
        axis=1,
    )
    for i in range(out.shape[0]):
        out[i] = value


def project_kernel(got, gram, out):
    h = gram.shape[0]
    n = 3 * h
    new = got[0]
    for i in range(1, got.shape[0]):
        new = new + got[i]
    old = gram[...]
    zero = jnp.zeros((h, h), F32)
    unit = jnp.where(iota((n, n), 0) == iota((n, n), 1), 1.0, 0.0)

    def whole(xx, xp, pp, wx, ww, wp):
        upper = jnp.concatenate(
            [
                jnp.concatenate([0.5 * xx, zero, xp], axis=1),
                jnp.concatenate([wx, 0.5 * ww, wp], axis=1),
                jnp.concatenate([zero, zero, 0.5 * pp], axis=1),
            ],
            axis=0,
        )
        return upper + nt(unit, upper, EXACT)

    def piece(a, i):
        return a[:, i * h : (i + 1) * h]

    gram_b = whole(
        piece(old, 0), piece(old, 1), piece(old, 2), piece(new, 0), piece(new, 2), piece(new, 1)
    )
    gram_a = whole(
        piece(old, 3), piece(old, 4), piece(old, 5), piece(new, 3), piece(new, 5), piece(new, 4)
    )
    unit_row, unit_col = unit_scales(gram_b)
    inverse = invert_dense(gram_b * unit_row * unit_col, False) * unit_row
    out[...] = nt(nn(inverse, gram_a, EXACT), inverse, EXACT)


def body(self_tiles, link_tiles, links, coarse_row, vectors, directions):
    count, size = self_tiles.shape[0], self_tiles.shape[1]
    mine = vectors.shape[0]
    slab = count * size
    vec = lax.axis_size("vec")
    k = mine * vec
    row_axes = ("z", "y", "core")
    row_index = lax.axis_index(row_axes)
    row_count = lax.axis_size(row_axes)
    stage_one = ("z", "core")
    n_one = lax.axis_size(stage_one)
    n_two = lax.axis_size("y")
    forward = [(i, i + 1) for i in range(row_count - 1)]
    backward = [(i + 1, i) for i in range(row_count - 1)]

    def halo(a):
        return lax.ppermute(a, row_axes, forward), lax.ppermute(a, row_axes, backward)

    start_s = jnp.stack([row_index * count, lax.axis_index("vec")]).astype(jnp.int32)
    links_s = links.T
    both = run(stack_kernel, (vectors, directions), arr((vec, 2 * mine, slab)))
    both, start_s = lax.optimization_barrier((both, start_s))
    both = lax.all_to_all(both, "vec", 0, 0)
    self_far = pltpu.with_memory_space_constraint(self_tiles, pltpu.HBM)
    nodes, col, info, link_v = run(
        prep_kernel,
        (
            links_s, coarse_row, start_s,
            self_far,
            pltpu.with_memory_space_constraint(link_tiles, pltpu.HBM),
        ),
        (
            arr((8, slab)), arr((4, count, size)), arr((count, LANE)),
            arr(link_tiles.shape, BF16),
        ),
        scratch=(pltpu.VMEM(self_tiles.shape, BF16), pltpu.SemaphoreType.DMA((2 * count,))),
        smem=3,
        hbm=(3, 4),
    )
    fc = run(pack_kernel, (both, nodes), arr((2 * k + 8, slab)))
    fl, fh = halo(fc)
    ic, ip, gram = run(
        image_kernel,
        (links_s, start_s, self_far, link_v, fc, fl, fh),
        (arr((k, slab)), arr((k, slab)), arr((k, LANE))),
        scratch=(
            pltpu.VMEM((3 * count, 2 * k, size), BF16),
            pltpu.VMEM(self_tiles.shape, BF16),
            pltpu.SemaphoreType.DMA,
        ),
        smem=2,
        hbm=(2,),
    )
    il, ih = halo(ic)
    sent = run(
        restrict_kernel,
        (links_s, start_s, fc, fl, fh, ic, il, ih, col, gram, info),
        arr((n_one, 2 * count, LANE)),
        scratch=(
            pltpu.VMEM((3 * count, 2 * k, size), F32),
            pltpu.VMEM((count * 2 * k, size), F32),
            pltpu.VMEM((2 * count, LANE), F32),
        ),
        smem=2,
    )
    got = lax.all_to_all(sent, stage_one, 0, 0)
    depth = count * (3 + n_one // GROUPS)
    sent = run(
        relay_kernel,
        (got,),
        arr((n_two, depth, LANE)),
        scratch=(pltpu.VMEM((depth, LANE), F32),),
    )
    got = lax.all_to_all(sent, "y", 0, 0)
    coarse_count = coarse_row.shape[0] // 2
    blocks = n_two * (n_one // GROUPS) * count
    coef, gain, gram = run(
        coarse_kernel,
        (coarse_row, start_s, got),
        (arr((k, k)), arr((k, 32)), arr((k, LANE))),
        scratch=(
            pltpu.VMEM((blocks, LANE), F32),
            pltpu.VMEM((blocks, LANE), F32),
            pltpu.VMEM((coarse_count, coarse_count), F32),
            pltpu.VMEM((GROUPS, blocks, coarse_count), BF16),
            pltpu.VMEM((coarse_count, coarse_count), F32),
            pltpu.VMEM((coarse_count, min(LANE, coarse_count)), F32),
        ),
        smem=2,
    )
    residual, my_corrected, corrected, scaled = run(
        correct_kernel,
        (links_s, start_s, self_tiles, link_v, fc, fl, fh, ic, il, ih, coef, gain),
        (arr((mine, slab)), arr((mine, slab)), arr((k, slab)), arr((k, slab), BF16)),
        scratch=(
            pltpu.VMEM((3 * count, k, size), BF16),
            pltpu.VMEM((k, slab), F32),
            pltpu.VMEM((k, slab), F32),
        ),
        smem=2,
    )
    sl, sh = halo(scaled)
    sent = run(
        search_kernel,
        (links_s, start_s, self_tiles, link_v, corrected, scaled, sl, sh, fc, ic, ip),
        arr((n_one, k, LANE)),
        scratch=(pltpu.VMEM((3 * count, k, size), BF16), pltpu.VMEM((k, slab), F32)),
        smem=2,
    )
    got = lax.all_to_all(sent, stage_one, 0, 0)
    sent = run(add_kernel, (got,), arr((n_two, k, LANE)))
    got = lax.all_to_all(sent, "y", 0, 0)
    projected = run(project_kernel, (got, gram), arr((3 * k, 3 * k)))
    return residual, my_corrected, projected


def row_split(rows):
    return (8, rows // 16, 2) if rows >= 64 else (2, rows // 4, 2)


def solution(mesh):
    z, y, core = row_split(mesh.shape["rows"])
    split = Mesh(
        mesh.devices.reshape(z, y, core, mesh.shape["vec"]), ("z", "y", "core", "vec")
    )
    rows = ("z", "y", "core")
    in_specs = (
        P(rows, None, None),
        P(rows, None, None, None),
        P(),
        P(),
        P("vec", rows),
        P("vec", rows),
    )
    out_specs = (P("vec", rows), P("vec", rows), P())
    return jax.shard_map(body, mesh=split, in_specs=in_specs, out_specs=out_specs, check_vma=False)
```

```python
import functools
import jax
import jax.numpy as jnp
from jax import lax
from jax.experimental import pallas as pl
from jax.experimental.pallas import tpu as pltpu
from jax.sharding import Mesh, PartitionSpec as P

spectral_shift = 0.25
damping = 0.6
LANE = 128
GROUPS = 4

F32 = jnp.float32
BF16 = jnp.bfloat16
EXACT = lax.Precision.HIGHEST


def nn(left, right, precision=None):
    return lax.dot_general(
        left, right, (((1,), (0,)), ((), ())), precision=precision, preferred_element_type=F32
    )


def nt(left, right, precision=None):
    return lax.dot_general(
        left, right, (((1,), (1,)), ((), ())), precision=precision, preferred_element_type=F32
    )


def tn(left, right, precision=None):
    return lax.dot_general(
        left, right, (((0,), (0,)), ((), ())), precision=precision, preferred_element_type=F32
    )


def iota(shape, dim):
    return lax.broadcasted_iota(jnp.int32, shape, dim)


def run(kernel, inputs, outputs, scratch=(), smem=0, hbm=()):
    in_specs = [
        pl.BlockSpec(
            memory_space=pltpu.SMEM if i < smem else pltpu.HBM if i in hbm else pltpu.VMEM
        )
        for i in range(len(inputs))
    ]
    single = not isinstance(outputs, (list, tuple))
    shapes = [outputs] if single else list(outputs)
    specs = [pl.BlockSpec(memory_space=pltpu.VMEM) for _ in shapes]
    return pl.pallas_call(
        kernel,
        in_specs=in_specs,
        out_specs=specs[0] if single else specs,
        out_shape=shapes[0] if single else shapes,
        scratch_shapes=list(scratch),
        compiler_params=pltpu.CompilerParams(vmem_limit_bytes=16 << 20),
    )(*inputs)


def arr(shape, dtype=F32):
    return jax.ShapeDtypeStruct(shape, dtype)


def safe(value):
    return jnp.where(value > 0.0, value, 1.0)


def stack_kernel(far_vectors, far_directions, out, vectors, directions, arrived):
    mine = vectors.shape[0]
    first = pltpu.make_async_copy(far_vectors, vectors, arrived.at[0])
    second = pltpu.make_async_copy(far_directions, directions, arrived.at[1])
    first.start()
    second.start()
    first.wait()
    second.wait()
    for v in range(out.shape[0]):
        out[v, :mine] = vectors[...]
        out[v, mine:] = directions[...]


def prep_kernel(
    links_s, coarse_s, start_s, self_far, link_far, nodes, col, info, link_t, self_t, arrived
):
    count, size = self_t.shape[0], self_t.shape[1]
    copies = []
    for b in range(count):
        copies.append(pltpu.make_async_copy(self_far.at[b], self_t.at[b], arrived.at[b]))
        copies.append(pltpu.make_async_copy(link_far.at[b], link_t.at[b], arrived.at[count + b]))
    for copy in copies:
        copy.start()
    ones = jnp.ones((8, size), BF16)
    diagonal = iota((size, size), 0) == iota((size, size), 1)
    lane = iota((1, LANE), 1)
    for b in range(count):
        copies[2 * b].wait()
        copies[2 * b + 1].wait()
        own = self_t[b]
        degree = nt(ones, own)[0:1]
        col[0, b : b + 1, :] = degree
        row = jnp.where(lane == 0, jnp.sum(degree, axis=1, keepdims=True), 0.0)
        ids = jnp.where(lane == 4, coarse_s[start_s[0] + b], 0)
        for s in range(3):
            tile = link_t[b, s]
            part = nt(ones, tile)[0:1]
            degree = degree + part
            row = jnp.where(lane == 1 + s, jnp.sum(part, axis=1, keepdims=True), row)
            ids = jnp.where(lane == 5 + s, coarse_s[links_s[s, start_s[0] + b]], ids)
            col[1 + s, b : b + 1, :] = jnp.sum(tile.astype(F32), axis=0, keepdims=True)
        diag = jnp.sum(jnp.where(diagonal, own.astype(F32), 0.0), axis=0, keepdims=True)
        span = slice(b * size, (b + 1) * size)
        nodes[0:1, span] = degree
        nodes[1:2, span] = 1.0 + spectral_shift - diag / degree
        info[b : b + 1, :] = row + ids.astype(F32)
    nodes[2:8, :] = jnp.zeros((6, nodes.shape[1]), F32)


def pack_kernel(both, nodes, out):
    members, twice, _ = both.shape
    mine = twice // 2
    for v in range(members):
        out[v * mine : (v + 1) * mine, :] = both[v, :mine]
        out[(members + v) * mine : (members + v + 1) * mine, :] = both[v, mine:]
    out[members * twice :, :] = nodes[...]


def linked(links_s, start_s, b, s, count):
    return links_s[s, start_s[0] + b] - start_s[0] + count


def apply_tiles(links_s, start_s, self_t, link_t, win, b, count):
    acc = nt(win[count + b], self_t[b])
    for s in range(3):
        acc = acc + nt(win[linked(links_s, start_s, b, s, count)], link_t[b, s])
    return acc


def image_kernel(
    links_s, start_s, self_far, link_t, fc, fl, fh, image_x, image_p, gram, win, self_t, arrived
):
    count, size = self_t.shape[0], self_t.shape[1]
    copy = pltpu.make_async_copy(self_far, self_t, arrived)
    copy.start()
    half = image_x.shape[0]
    both = 2 * half
    for part, f in enumerate((fl, fc, fh)):
        for b in range(count):
            span = slice(b * size, (b + 1) * size)
            root = jnp.sqrt(safe(f[both : both + 1, span]))
            win[part * count + b] = (f[:both, span] / root).astype(BF16)
    copy.wait()
    for b in range(count):
        acc = apply_tiles(links_s, start_s, self_t, link_t, win, b, count)
        span = slice(b * size, (b + 1) * size)
        value = fc[:both, span] - acc / jnp.sqrt(fc[both : both + 1, span])
        image_x[:, span] = value[:half]
        image_p[:, span] = value[half:]
    z = fc[:both, :]
    ix = image_x[...]
    ip = image_p[...]
    basis = nt(z, z, EXACT)
    cross = nt(ix, z, EXACT)
    other = nt(ip, z, EXACT)
    mixed = 0.5 * (cross[:, half:] + nt(z[:half], ip, EXACT))
    gram[:, 0:half] = basis[:half, :half]
    gram[:, half : 2 * half] = basis[:half, half:]
    gram[:, 2 * half : 3 * half] = basis[half:, half:]
    gram[:, 3 * half : 4 * half] = cross[:, :half]
    gram[:, 4 * half : 5 * half] = mixed
    gram[:, 5 * half : 6 * half] = other[:, half:]
    gram[:, 6 * half :] = jnp.zeros((half, LANE - 6 * half), F32)


def node_scales(f, both, span):
    shift = f[both + 1 : both + 2, span]
    return jnp.sqrt(safe(f[both : both + 1, span])), jnp.where(shift == 0.0, 1.0, shift)


def restrict_kernel(
    links_s, start_s, fc, fl, fh, ic, il, ih, col, gram, info, out, win, weighted, packed
):
    count, size = col.shape[1], col.shape[2]
    half = ic.shape[0]
    width = 2 * half
    for part, (f, img) in enumerate(((fl, il), (fc, ic), (fh, ih))):
        for b in range(count):
            span = slice(b * size, (b + 1) * size)
            root, shift = node_scales(f, width, span)
            field = jnp.concatenate([f[:half, span], img[:, span]], axis=0)
            smooth = field * (damping / shift)
            win[part * count + b] = smooth / root
            if part == 1:
                weighted[b * width : (b + 1) * width, :] = root * (
                    field - (1.0 + spectral_shift) * smooth
                )
    for b in range(count):
        acc = weighted[b * width : (b + 1) * width, :] + col[0, b : b + 1, :] * win[count + b]
        for s in range(3):
            acc = acc + col[1 + s, b : b + 1, :] * win[linked(links_s, start_s, b, s, count)]
        weighted[b * width : (b + 1) * width, :] = acc
    sums = nt(jnp.ones((8, size), F32), weighted[...], EXACT)
    packed[...] = gram[...]
    for b in range(count):
        packed[b : b + 1, LANE - width :] = sums[0:1, b * width : (b + 1) * width]
        packed[count + b : count + b + 1, LANE - width :] = info[b : b + 1, 0:width]
    value = packed[...]
    for i in range(out.shape[0]):
        out[i] = value


def relay_kernel(got, out, packed):
    members, rows, _ = got.shape
    half = rows // 2
    deep = members // GROUPS
    width = LANE // GROUPS
    total = got[0]
    for i in range(1, members):
        total = total + got[i]
    packed[0:rows, :] = total
    tail = rows + deep * half
    if members * 8 < LANE:
        packed[tail : tail + half, :] = jnp.zeros((half, LANE), F32)
    for i in range(members):
        g, j = i // deep, i % deep
        at = rows + j * half
        mine = got[i]
        packed[at : at + half, g * width : (g + 1) * width] = mine[:half, LANE - width :]
        packed[tail : tail + half, i * 8 : (i + 1) * 8] = mine[half:, LANE - width : LANE - width + 8]
    value = packed[...]
    for i in range(out.shape[0]):
        out[i] = value


def add_kernel(got, out):
    total = got[0]
    for i in range(1, got.shape[0]):
        total = total + got[i]
    for i in range(out.shape[0]):
        out[i] = total


def lane_copy(tile, at):
    return jnp.broadcast_to(tile[:, at : at + 1], tile.shape)


def row_copy(tile, at):
    return jnp.broadcast_to(tile[at : at + 1, :], tile.shape)


def solve_tile(cols, tile, more, sub):
    fields = list(cols) + [tile] + list(more)
    final = tile
    for p in range(0, 8, 2):
        q = p + 1
        vp, vq = fields[p], fields[q]
        a, c = row_copy(vp, p), row_copy(vp, q)
        b, d = row_copy(vq, p), row_copy(vq, q)
        det = a * d - b * c
        r = 1.0 / det
        ar, br, cr, dr = a * r, b * r, c * r, d * r
        f0, f1 = vp * dr - vq * cr, vq * ar - vp * br
        f0 = jnp.where(sub == p, 1.0 - dr, jnp.where(sub == q, cr, f0))
        f1 = jnp.where(sub == p, br, jnp.where(sub == q, 1.0 - ar, f1))
        x0, x1 = row_copy(fields[8], p), row_copy(fields[8], q)
        root = 1.0 / jnp.sqrt(a)
        final = jnp.where(sub == p, x0 * root, final)
        final = jnp.where(sub == q, (x1 * a - c * x0) * (root / jnp.sqrt(det)), final)
        for m in range(q + 1, len(fields)):
            x = fields[m]
            fields[m] = x - (f0 * row_copy(x, p) + f1 * row_copy(x, q))
    return fields[8], final, fields[9:]


def sum8(terms):
    a, b, c, d, e, f, g, h = terms
    return ((a + b) + (c + d)) + ((e + f) + (g + h))


def invert_dense(matrix, whole):
    n = matrix.shape[0]
    shape = (8, n)
    tiles = [matrix[8 * i : 8 * i + 8, :] for i in range(n // 8)]
    lane, sub = iota(shape, 1), iota(shape, 0)
    cols = [lane_copy(tiles[0], j) for j in range(8)]
    for at in range(n // 8):
        k = 8 * at
        last = at + 1 == n // 8
        inside = (lane >= k) & (lane < k + 8)
        start = jnp.where(inside, jnp.where(lane == sub + k, 1.0, 0.0), tiles[at])
        ahead = [] if last else [lane_copy(tiles[at], k + 8 + j) for j in range(8)]
        new, final, ahead = solve_tile(cols, start, ahead, sub)
        rows = [row_copy(new, j) for j in range(8)]
        for i in range(0 if whole else at + 1, n // 8):
            if i != at:
                old = tiles[i]
                parts = [lane_copy(old, k + j) for j in range(8)]
                if i == at + 1:
                    cols = [
                        lane_copy(old, k + 8 + j)
                        - sum8([parts[m] * row_copy(ahead[j], m) for m in range(8)])
                        for j in range(8)
                    ]
                tiles[i] = jnp.where(inside, 0.0, old) - sum8(
                    [parts[j] * rows[j] for j in range(8)]
                )
        tiles[at] = new if whole else jnp.where(lane <= sub + k, final, 0.0)
    return jnp.concatenate(tiles, axis=0)


def unit_scales(matrix):
    square = iota(matrix.shape, 0) == iota(matrix.shape, 1)
    diag = jnp.where(square, matrix, 0.0)
    row = 1.0 / jnp.sqrt(jnp.sum(diag, axis=0, keepdims=True))
    return row, 1.0 / jnp.sqrt(jnp.sum(diag, axis=1, keepdims=True))


def split3(value):
    high = value.astype(BF16)
    rest = value - high.astype(F32)
    mid = rest.astype(BF16)
    low = (rest - mid.astype(F32)).astype(BF16)
    return high, mid, low


def coarse_kernel(coarse_s, start_s, got, coef, gain, gram, uw, info, mat, hot, upper, pivots):
    members, depth, _ = got.shape
    rows = 16
    half = rows
    deep = (depth - rows) // 8 - 1
    width = LANE // GROUPS
    nc = mat.shape[0]
    count = coarse_s.shape[0]
    total = got[0, 0:rows]
    for y in range(1, members):
        total = total + got[y, 0:rows]
    gram[...] = total
    for y in range(members):
        for j in range(deep):
            at = (y * deep + j) * 8
            src = rows + j * 8
            uw[at : at + 8, :] = got[y, src : src + 8]
            for g in range(GROUPS):
                i = (g * deep + j) * 8
                info[at : at + 8, g * width : g * width + 8] = got[y, depth - 8 :, i : i + 8]
    blocks = uw.shape[0]
    lanes = iota((blocks, nc), 1)
    agg = jnp.zeros((1, nc), F32)
    tiles = jnp.zeros((nc, nc), F32)
    for g in range(GROUPS):
        at = g * width
        values = [info[:, at + s : at + s + 1] for s in range(4)]
        ids = [info[:, at + 4 + s : at + 5 + s].astype(jnp.int32) for s in range(4)]
        here = lanes == ids[0]
        block_degree = values[0] + values[1] + values[2] + values[3]
        agg = agg + jnp.sum(jnp.where(here, block_degree, 0.0), axis=0, keepdims=True)
        spread = jnp.where(here, values[0], 0.0)
        for s in range(1, 4):
            spread = spread + jnp.where(lanes == ids[s], values[s], 0.0)
        member = jnp.where(here, 1.0, 0.0).astype(BF16)
        hot[g] = member
        pieces = tn(member, jnp.concatenate(split3(spread), axis=1))
        tiles = tiles + (pieces[:, :nc] + (pieces[:, nc : 2 * nc] + pieces[:, 2 * nc :]))
    same = iota((nc, nc), 0) == iota((nc, nc), 1)
    agg_col = jnp.sum(jnp.where(same, agg, 0.0), axis=1, keepdims=True)
    inv_row = 1.0 / jnp.sqrt(agg)
    inv_col = 1.0 / jnp.sqrt(agg_col)
    mat[...] = (jnp.where(same, (1.0 + spectral_shift) * agg, 0.0) - tiles) * inv_col * inv_row

    grams = total[:, 0:half]
    square = iota((half, half), 0) == iota((half, half), 1)
    unit_row, unit_col = unit_scales(grams)
    inverse = invert_dense(grams * unit_row * unit_col, True) * unit_row * unit_col
    ritz = nn(total[:, 3 * half : 4 * half], inverse, EXACT)
    coef[...] = ritz
    combine = jnp.concatenate([-ritz, jnp.where(square, 1.0, 0.0)], axis=1)
    rhs = jnp.zeros((half, nc), F32)
    for g in range(GROUPS):
        block_rhs = nt(combine, uw[:, g * width : (g + 1) * width], EXACT)
        pieces = nn(jnp.concatenate(split3(block_rhs), axis=0), hot[g])
        rhs = rhs + (pieces[:half] + (pieces[half : 2 * half] + pieces[2 * half :]))
    rhs = rhs * inv_row

    block = min(LANE, nc)
    steps = nc // block

    def eliminate(step, _):
        at = pl.multiple_of(step * block, block)
        pivot = invert_dense(mat[pl.ds(at, block), pl.ds(at, block)], False)
        pivots[pl.ds(at, block), :] = pivot
        for j in range(steps - 1):

            @pl.when(step == j)
            def _():
                lo, hi = j * block, (j + 1) * block
                strip = nn(pivot, mat[lo:hi, hi:], EXACT)
                upper[lo:hi, hi:] = strip
                mat[hi:, hi:] = mat[hi:, hi:] - tn(strip, strip, EXACT)

        return 0

    lax.fori_loop(0, steps, eliminate, 0)
    halves = []
    for j in range(steps):
        lo, hi = j * block, (j + 1) * block
        head = nt(rhs[:, :block], pivots[lo:hi, :], EXACT)
        halves.append(head)
        if hi < nc:
            rhs = rhs[:, block:] - nn(head, upper[lo:hi, hi:], EXACT)
    error = nn(halves[-1], pivots[nc - block :, :], EXACT)
    for j in reversed(range(steps - 1)):
        lo, hi = j * block, (j + 1) * block
        head = halves[j] - nt(error, upper[lo:hi, hi:], EXACT)
        error = jnp.concatenate([nn(head, pivots[lo:hi, :], EXACT), error], axis=1)
    lifted = error * inv_row
    wide = iota((1, nc), 1)
    picks = []
    for j in range(24):
        at = jnp.clip(start_s[0] - 8 + j, 0, count - 1)
        picks.append(jnp.where(wide == coarse_s[at], 1.0, 0.0))
    picks.append(jnp.zeros((8, nc), F32))
    gain[...] = nt(lifted, jnp.concatenate(picks, axis=0), EXACT)


def correct_kernel(
    links_s, start_s, self_t, link_t, fc, fl, fh, ic, il, ih, coef, gain,
    my_residual, my_corrected, corrected, scaled, win, second, residual,
):
    count, size = self_t.shape[0], self_t.shape[1]
    half = ic.shape[0]
    both = 2 * half
    ritz = coef[...]
    gains = gain[...]
    for part, (f, img) in enumerate(((fl, il), (fc, ic), (fh, ih))):
        res = img[...] - nn(ritz, f[:half, :], EXACT)
        if part == 1:
            residual[...] = res
        for b in range(count):
            span = slice(b * size, (b + 1) * size)
            root, shift = node_scales(f, both, span)
            j = part * count + b
            field = damping * res[:, span] / shift + root * gains[:, j : j + 1]
            win[j] = (field / root).astype(BF16)
            if part == 1:
                second[:, span] = field
    for b in range(count):
        span = slice(b * size, (b + 1) * size)
        root, shift = node_scales(fc, both, span)
        acc = apply_tiles(links_s, start_s, self_t, link_t, win, b, count)
        field = second[:, span]
        after = field - acc / root + spectral_shift * field
        field = field + damping * (residual[:, span] - after) / shift
        corrected[:, span] = field
        scaled[:, span] = (field / root).astype(BF16)
    mine = my_residual.shape[0]
    pick = iota((mine, half), 1) == iota((mine, half), 0) + start_s[1] * mine
    pick = jnp.where(pick, 1.0, 0.0)
    my_residual[...] = nn(pick, residual[...], EXACT)
    my_corrected[...] = nn(pick, corrected[...], EXACT)


def search_kernel(links_s, start_s, self_t, link_t, w, sc, sl, sh, fc, ix, ip, out, win, image_w):
    count, size = self_t.shape[0], self_t.shape[1]
    half = w.shape[0]
    for part, s in enumerate((sl, sc, sh)):
        for b in range(count):
            win[part * count + b] = s[:, b * size : (b + 1) * size]
    for b in range(count):
        span = slice(b * size, (b + 1) * size)
        acc = apply_tiles(links_s, start_s, self_t, link_t, win, b, count)
        image_w[:, span] = w[:, span] - acc / jnp.sqrt(fc[2 * half : 2 * half + 1, span])
    field = w[...]
    field_image = image_w[...]
    zz = fc[: 2 * half, :]
    images = jnp.concatenate([ix[...], ip[...]], axis=0)
    value = jnp.concatenate(
        [
            nt(field, zz, EXACT),
            nt(field, field, EXACT),
            0.5 * (nt(field, images, EXACT) + nt(field_image, zz, EXACT)),
            nt(field, field_image, EXACT),
            jnp.zeros((half, LANE - 6 * half), F32),
        ],
        axis=1,
    )
    for i in range(out.shape[0]):
        out[i] = value


def project_kernel(got, gram, out):
    h = gram.shape[0]
    n = 3 * h
    new = got[0]
    for i in range(1, got.shape[0]):
        new = new + got[i]
    old = gram[...]
    zero = jnp.zeros((h, h), F32)
    unit = jnp.where(iota((n, n), 0) == iota((n, n), 1), 1.0, 0.0)

    def whole(xx, xp, pp, wx, ww, wp):
        upper = jnp.concatenate(
            [
                jnp.concatenate([0.5 * xx, zero, xp], axis=1),
                jnp.concatenate([wx, 0.5 * ww, wp], axis=1),
                jnp.concatenate([zero, zero, 0.5 * pp], axis=1),
            ],
            axis=0,
        )
        return upper + nt(unit, upper, EXACT)

    def piece(a, i):
        return a[:, i * h : (i + 1) * h]

    gram_b = whole(
        piece(old, 0), piece(old, 1), piece(old, 2), piece(new, 0), piece(new, 2), piece(new, 1)
    )
    gram_a = whole(
        piece(old, 3), piece(old, 4), piece(old, 5), piece(new, 3), piece(new, 5), piece(new, 4)
    )
    unit_row, unit_col = unit_scales(gram_b)
    inverse = invert_dense(gram_b * unit_row * unit_col, False) * unit_row
    out[...] = nt(nn(inverse, gram_a, EXACT), inverse, EXACT)


def body(self_tiles, link_tiles, links, coarse_row, vectors, directions):
    count, size = self_tiles.shape[0], self_tiles.shape[1]
    mine = vectors.shape[0]
    slab = count * size
    vec = lax.axis_size("vec")
    k = mine * vec
    row_axes = ("z", "y", "core")
    row_index = lax.axis_index(row_axes)
    row_count = lax.axis_size(row_axes)
    stage_one = ("z", "core")
    n_one = lax.axis_size(stage_one)
    n_two = lax.axis_size("y")
    forward = [(i, i + 1) for i in range(row_count - 1)]
    backward = [(i + 1, i) for i in range(row_count - 1)]

    def halo(a):
        return lax.ppermute(a, row_axes, forward), lax.ppermute(a, row_axes, backward)

    start_s = jnp.stack([row_index * count, lax.axis_index("vec")]).astype(jnp.int32)
    links_s = links.T
    both = run(
        stack_kernel,
        (
            pltpu.with_memory_space_constraint(vectors, pltpu.HBM),
            pltpu.with_memory_space_constraint(directions, pltpu.HBM),
        ),
        arr((vec, 2 * mine, slab)),
        scratch=(
            pltpu.VMEM((mine, slab), F32),
            pltpu.VMEM((mine, slab), F32),
            pltpu.SemaphoreType.DMA((2,)),
        ),
        hbm=(0, 1),
    )
    both, start_s = lax.optimization_barrier((both, start_s))
    both = lax.all_to_all(both, "vec", 0, 0)
    self_far = pltpu.with_memory_space_constraint(self_tiles, pltpu.HBM)
    nodes, col, info, link_v = run(
        prep_kernel,
        (
            links_s, coarse_row, start_s,
            self_far,
            pltpu.with_memory_space_constraint(link_tiles, pltpu.HBM),
        ),
        (
            arr((8, slab)), arr((4, count, size)), arr((count, LANE)),
            arr(link_tiles.shape, BF16),
        ),
        scratch=(pltpu.VMEM(self_tiles.shape, BF16), pltpu.SemaphoreType.DMA((2 * count,))),
        smem=3,
        hbm=(3, 4),
    )
    fc = run(pack_kernel, (both, nodes), arr((2 * k + 8, slab)))
    fl, fh = halo(fc)
    ic, ip, gram = run(
        image_kernel,
        (links_s, start_s, self_far, link_v, fc, fl, fh),
        (arr((k, slab)), arr((k, slab)), arr((k, LANE))),
        scratch=(
            pltpu.VMEM((3 * count, 2 * k, size), BF16),
            pltpu.VMEM(self_tiles.shape, BF16),
            pltpu.SemaphoreType.DMA,
        ),
        smem=2,
        hbm=(2,),
    )
    il, ih = halo(ic)
    sent = run(
        restrict_kernel,
        (links_s, start_s, fc, fl, fh, ic, il, ih, col, gram, info),
        arr((n_one, 2 * count, LANE)),
        scratch=(
            pltpu.VMEM((3 * count, 2 * k, size), F32),
            pltpu.VMEM((count * 2 * k, size), F32),
            pltpu.VMEM((2 * count, LANE), F32),
        ),
        smem=2,
    )
    got = lax.all_to_all(sent, stage_one, 0, 0)
    depth = count * (3 + n_one // GROUPS)
    sent = run(
        relay_kernel,
        (got,),
        arr((n_two, depth, LANE)),
        scratch=(pltpu.VMEM((depth, LANE), F32),),
    )
    got = lax.all_to_all(sent, "y", 0, 0)
    coarse_count = coarse_row.shape[0] // 2
    blocks = n_two * (n_one // GROUPS) * count
    coef, gain, gram = run(
        coarse_kernel,
        (coarse_row, start_s, got),
        (arr((k, k)), arr((k, 32)), arr((k, LANE))),
        scratch=(
            pltpu.VMEM((blocks, LANE), F32),
            pltpu.VMEM((blocks, LANE), F32),
            pltpu.VMEM((coarse_count, coarse_count), F32),
            pltpu.VMEM((GROUPS, blocks, coarse_count), BF16),
            pltpu.VMEM((coarse_count, coarse_count), F32),
            pltpu.VMEM((coarse_count, min(LANE, coarse_count)), F32),
        ),
        smem=2,
    )
    residual, my_corrected, corrected, scaled = run(
        correct_kernel,
        (links_s, start_s, self_tiles, link_v, fc, fl, fh, ic, il, ih, coef, gain),
        (arr((mine, slab)), arr((mine, slab)), arr((k, slab)), arr((k, slab), BF16)),
        scratch=(
            pltpu.VMEM((3 * count, k, size), BF16),
            pltpu.VMEM((k, slab), F32),
            pltpu.VMEM((k, slab), F32),
        ),
        smem=2,
    )
    sl, sh = halo(scaled)
    sent = run(
        search_kernel,
        (links_s, start_s, self_tiles, link_v, corrected, scaled, sl, sh, fc, ic, ip),
        arr((n_one, k, LANE)),
        scratch=(pltpu.VMEM((3 * count, k, size), BF16), pltpu.VMEM((k, slab), F32)),
        smem=2,
    )
    got = lax.all_to_all(sent, stage_one, 0, 0)
    sent = run(add_kernel, (got,), arr((n_two, k, LANE)))
    got = lax.all_to_all(sent, "y", 0, 0)
    projected = run(project_kernel, (got, gram), arr((3 * k, 3 * k)))
    return residual, my_corrected, projected


def row_split(rows):
    return (8, rows // 16, 2) if rows >= 64 else (2, rows // 4, 2)


def solution(mesh):
    z, y, core = row_split(mesh.shape["rows"])
    split = Mesh(
        mesh.devices.reshape(z, y, core, mesh.shape["vec"]), ("z", "y", "core", "vec")
    )
    rows = ("z", "y", "core")
    in_specs = (
        P(rows, None, None),
        P(rows, None, None, None),
        P(),
        P(),
        P("vec", rows),
        P("vec", rows),
    )
    out_specs = (P("vec", rows), P("vec", rows), P())
    return jax.shard_map(body, mesh=split, in_specs=in_specs, out_specs=out_specs, check_vma=False)
```
